512 devices in a mesh: seq: 64 (over x, z), head: 8 (over y, core).
Axes of the slice: x: 4, y: 4, z: 16, core: 2. Of those that a mesh axis runs over, the one named last changes fastest.
Arguments:
- query_raw: bfloat16 [24576, 2048], P('seq', 'head'), may hold values from -6 to 6
- key_raw: bfloat16 [24576, 2048], P('seq', 'head'), may hold values from -6 to 6
- value_raw: bfloat16 [24576, 4096], P('seq', 'head'), may hold values from -6 to 6
- gate_raw: bfloat16 [24576, 4096], P('seq', 'head'), may hold values from -6 to 6
- query_taps: float32 [4, 2048], P(None, 'head'), may hold values from -3 to 3
- key_taps: float32 [4, 2048], P(None, 'head'), may hold values from -3 to 3
- value_taps: float32 [4, 4096], P(None, 'head'), may hold values from -3 to 3
- beta_logit: float32 [24576, 32], P('seq', 'head'), may hold values from -6 to 6
- decay_logit: float32 [24576, 32], P('seq', 'head'), may hold values from -14 to 0
- norm_gain: float32 [128], replicated, may hold values from 0.5 to 1.5
- out_weight: bfloat16 [4096, 2048], P('head'), may hold values from -0.09375 to 0.09375
Outputs:
- mixed: bfloat16 [24576, 2048], P(('seq', 'head'))
The draws below stay inside these ranges and needn't reach their ends.
All inputs are finite; a program needn't handle non-finite values.
Results may differ from the reference program's by a relative error of at most 0.017.
Values may be sent and summed in bfloat16 or wider, within the bound.
A program may use at most 128 MiB of HBM per device.

```python
import jax
import jax.numpy as jnp
from jax import lax

D = 2048
HK = 16
VALUE_HEADS = 32
DK = 128
DV = 128
BLOCK = 64
TOK_DEV = 384
WINDOW_TOKENS = 24576
N_HEAD = 8


def draw_key_raw(key, part):
    random_subkeys = jax.random.split(key, 2)
    channel_scale = jnp.exp(jax.random.uniform(random_subkeys[0], (HK * DK,), jnp.float32, jnp.log(0.001), 0.0))
    entries = jnp.clip(jax.random.normal(random_subkeys[1], (WINDOW_TOKENS, HK * DK), jnp.float32), -6.0, 6.0)
    return (entries * channel_scale).astype(jnp.bfloat16)


def draw_decay_logit(key, part):
    random_subkeys = jax.random.split(key, 7)
    fast_heads = jax.random.randint(random_subkeys[0], (VALUE_HEADS,), 0, 2) == 0
    slow_rate = jnp.exp(jax.random.uniform(random_subkeys[1], (VALUE_HEADS,), jnp.float32, jnp.log(0.15), jnp.log(0.6))) / WINDOW_TOKENS
    fast_rate = jnp.exp(jax.random.uniform(random_subkeys[2], (VALUE_HEADS,), jnp.float32, jnp.log(1.0 / 50.0), jnp.log(1.0 / 30.0)))
    base_rate = jnp.where(fast_heads, fast_rate, slow_rate)
    shards = WINDOW_TOKENS // TOK_DEV
    shard_factor = jnp.exp(jax.random.uniform(random_subkeys[3], (shards, 1, VALUE_HEADS), jnp.float32, jnp.log(0.5), 0.0))
    roughness = jax.random.uniform(random_subkeys[4], (shards, TOK_DEV, VALUE_HEADS), jnp.float32, 0.5, 1.5)
    decay_rates = (base_rate * shard_factor * roughness).reshape(WINDOW_TOKENS, VALUE_HEADS)
    spike_positions = jax.random.randint(random_subkeys[5], (3, VALUE_HEADS), 0, WINDOW_TOKENS)
    token_positions = jnp.arange(WINDOW_TOKENS, dtype=jnp.int32)
    spike_mask = jnp.any(token_positions[:, None, None] == spike_positions[None, :, :], axis=1)
    spike_rate = jax.random.uniform(random_subkeys[6], (WINDOW_TOKENS, VALUE_HEADS), jnp.float32, 0.22, 0.41)
    decay_rates = jnp.where(spike_mask, spike_rate, decay_rates)
    return jnp.log(jnp.expm1(decay_rates))


def block_scale(own_key, dims, cuts, least, largest):
    def one(position, parts):
        heights = jax.random.uniform(jax.random.fold_in(jax.random.fold_in(own_key, 6), position), (parts,), jnp.float32, least / len(cuts), largest / len(cuts))
        return jnp.repeat(jnp.exp(heights), dims[position] // parts).reshape((-1,) + (1,) * (len(dims) - position - 1))

    level = one(*cuts[0])
    for cut in cuts[1:]:
        level = level * one(*cut)
    return level


def normal_values(key, shape, scale, bound, cuts=(), kind=jnp.bfloat16):
    array = jax.random.normal(key, shape, jnp.float32) * scale
    if len(cuts) > 0:
        array = block_scale(key, shape, cuts, -0.22, 0.18) * array
    return jnp.clip(array, min=-bound, max=bound).astype(kind)


def setup_inputs(seed: int = 0) -> dict:
    keys = jax.random.split(jax.random.key(seed), 12)
    query_raw = normal_values(keys[0], (WINDOW_TOKENS, HK * DK), 1.0, 6.0, ((0, 64), (1, 8)))
    key_raw = draw_key_raw(jax.random.fold_in(keys[11], 71), 0)
    value_raw = normal_values(keys[2], (WINDOW_TOKENS, VALUE_HEADS * DV), 1.0, 6.0, ((0, 64), (1, 8)))
    gate_raw = normal_values(keys[3], (WINDOW_TOKENS, VALUE_HEADS * DV), 1.0, 6.0, ((0, 64), (1, 8)))
    query_taps = normal_values(keys[4], (4, HK * DK), 0.5, 3.0, ((1, 8),), jnp.float32)
    key_taps = normal_values(keys[5], (4, HK * DK), 0.5, 3.0, ((1, 8),), jnp.float32)
    value_taps = normal_values(keys[6], (4, VALUE_HEADS * DV), 0.5, 3.0, ((1, 8),), jnp.float32)
    beta_logit = normal_values(keys[7], (WINDOW_TOKENS, VALUE_HEADS), 1.5, 6.0, ((0, 64), (1, 8)), jnp.float32)
    decay_logit = draw_decay_logit(jax.random.fold_in(keys[11], 71), 0)
    norm_gain = jnp.clip(1.0 + 0.1 * jax.random.normal(keys[9], (DV,), jnp.float32), 0.5, 1.5)
    out_weight = normal_values(keys[10], (VALUE_HEADS * DV, D), (VALUE_HEADS * DV) ** -0.5, 0.09375, ((0, 8),))
    return {"query_raw": query_raw, "key_raw": key_raw, "value_raw": value_raw, "gate_raw": gate_raw, "query_taps": query_taps, "key_taps": key_taps, "value_taps": value_taps, "beta_logit": beta_logit, "decay_logit": decay_logit, "norm_gain": norm_gain, "out_weight": out_weight}


PRECISE = lax.Precision.HIGHEST
EPSILON = 1e-06

def conv_silu(raw_rows, before, weight):
    extended = jnp.concatenate([before, raw_rows], 0).astype(jnp.float32)
    length = raw_rows.shape[0]
    summed = weight[0] * extended[0:length]
    for offset in range(1, 4):
        summed = summed + weight[offset] * extended[offset:offset + length]
    return jax.nn.silu(summed)

def prepare(query_conv, key_conv, value_conv, beta_logit, decay_logit):
    length = query_conv.shape[0]
    head_keys = key_conv.shape[1] // DK
    head_values = value_conv.shape[1] // DV
    repeat_by = head_values // head_keys
    blocks = length // BLOCK
    key_three = key_conv.reshape(length, head_keys, DK)
    key_three = key_three * lax.rsqrt(lax.optimization_barrier(jnp.sum(key_three * key_three, -1, keepdims=True)) + EPSILON)
    query_three = query_conv.reshape(length, head_keys, DK)

    def arrange(array_in):
        moved = jnp.moveaxis(array_in, 1, 0)
        return moved.reshape((moved.shape[0], blocks, BLOCK) + moved.shape[2:])
    queries = arrange(jnp.repeat(query_three, repeat_by, axis=1))
    key_rows = arrange(jnp.repeat(key_three, repeat_by, axis=1))
    value_rows = arrange(value_conv.reshape(length, head_values, DV))
    decays = arrange(-jax.nn.softplus(decay_logit))
    beta_rows = arrange(jax.nn.sigmoid(beta_logit))
    return (queries, key_rows, value_rows, decays, beta_rows)

def stack_mul(left, right):
    return jnp.einsum('bkl,blv->bkv', left, right, precision=PRECISE)

def block_parts(queries, key_rows, value_rows, decays, beta_rows):
    block_len = decays.shape[-1]
    log_fade = jnp.cumsum(decays, axis=-1)
    row_ids = lax.broadcasted_iota(jnp.int32, (block_len, block_len), 0)
    col_ids = lax.broadcasted_iota(jnp.int32, (block_len, block_len), 1)
    gap_log = log_fade[..., :, None] - log_fade[..., None, :]
    strict = row_ids > col_ids
    within = row_ids >= col_ids
    decay_low = jnp.where(strict, jnp.exp(jnp.where(strict, gap_log, 0.0)), 0.0)
    decay_on = jnp.where(within, jnp.exp(jnp.where(within, gap_log, 0.0)), 0.0)
    key_inner = jnp.einsum('bik,bjk->bij', key_rows, key_rows, precision=PRECISE)
    system = jnp.eye(block_len, dtype=jnp.float32) + beta_rows[..., :, None] * decay_low * key_inner
    rhs_both = jnp.concatenate([beta_rows[..., None] * value_rows, (beta_rows * jnp.exp(log_fade))[..., None] * key_rows], -1)
    solved = lax.linalg.triangular_solve(system, rhs_both, left_side=True, lower=True, unit_diagonal=True)
    value_dim = value_rows.shape[-1]
    updates = solved[..., :value_dim]
    wide = solved[..., value_dim:]
    scores = decay_on * jnp.einsum('bik,bjk->bij', queries, key_rows, precision=PRECISE)
    tail_fade = jnp.exp(log_fade[..., -1:] - log_fade)
    faded_keys = key_rows * tail_fade[..., None]
    last_fade = jnp.exp(log_fade[..., -1])
    identity = jnp.eye(key_rows.shape[-1], dtype=jnp.float32)
    transit = last_fade[..., None, None] * identity - jnp.einsum('bck,bcl->bkl', faded_keys, wide, precision=PRECISE)
    inject = jnp.einsum('bck,bcv->bkv', faded_keys, updates, precision=PRECISE)
    return (updates, wide, scores, log_fade, transit, inject)

def block_out(queries, scores, log_fade, updates, wide, state_now):
    fresh = updates - jnp.einsum('bck,bkv->bcv', wide, state_now, precision=PRECISE)
    carried = jnp.einsum('bck,bkv->bcv', queries, state_now, precision=PRECISE)
    return jnp.exp(log_fade)[..., None] * carried + jnp.einsum('bij,bjv->biv', scores, fresh, precision=PRECISE)

def gated_norm(outputs, gate_raw, norm_gain):
    gate_three = gate_raw.reshape(outputs.shape).astype(jnp.float32)
    scale_rows = lax.rsqrt(lax.optimization_barrier(jnp.mean(outputs * outputs, -1, keepdims=True)) + EPSILON)
    normed = (outputs * scale_rows * norm_gain * jax.nn.silu(gate_three)).astype(jnp.bfloat16)
    return normed.reshape(outputs.shape[0], -1)

def reference(query_raw, key_raw, value_raw, gate_raw, query_taps, key_taps, value_taps, beta_logit, decay_logit, norm_gain, out_weight):
    query_conv = conv_silu(query_raw, jnp.zeros((3, query_raw.shape[1]), jnp.bfloat16), query_taps)
    key_conv = conv_silu(key_raw, jnp.zeros((3, key_raw.shape[1]), jnp.bfloat16), key_taps)
    value_conv = conv_silu(value_raw, jnp.zeros((3, value_raw.shape[1]), jnp.bfloat16), value_taps)
    prepared = prepare(query_conv, key_conv, value_conv, beta_logit, decay_logit)
    moved = tuple((jnp.moveaxis(array_in, 1, 0) for array_in in prepared))

    def block_step(state_now, pieces):
        updates, wide, scores, log_fade, transit, inject = block_parts(pieces[0], pieces[1], pieces[2], pieces[3], pieces[4])
        outputs = block_out(pieces[0], scores, log_fade, updates, wide, state_now)
        return (stack_mul(transit, state_now) + inject, outputs)
    initial = jnp.zeros((VALUE_HEADS, DK, DV), jnp.float32)
    _, outputs = lax.scan(block_step, initial, moved)
    core = jnp.moveaxis(outputs, 0, 1).reshape(VALUE_HEADS, -1, DV)
    core = jnp.moveaxis(core, 0, 1)
    normed = gated_norm(core, gate_raw, norm_gain)
    group_width = VALUE_HEADS * DV // N_HEAD
    summed = jnp.zeros((normed.shape[0], out_weight.shape[1]), jnp.float32)
    for part_index in range(N_HEAD):
        lower_col = part_index * group_width
        partial_value = jnp.dot(normed[:, lower_col:lower_col + group_width].astype(jnp.float32), out_weight[lower_col:lower_col + group_width].astype(jnp.float32), preferred_element_type=jnp.float32)
        summed = summed + lax.optimization_barrier(partial_value.astype(jnp.bfloat16)).astype(jnp.float32)
    return summed.astype(jnp.bfloat16)
```

```python
import functools
import jax, jax.numpy as jnp
from jax import lax
from jax.experimental import pallas as pl
from jax.experimental.pallas import tpu as pltpu
EPS=1e-6
F32=jnp.float32; BF=jnp.bfloat16
C=128
NC=3
def bdot(a,b):
    return lax.dot_general(a.astype(BF),b.astype(BF),(((1,),(0,)),((),())),preferred_element_type=F32)
def bdot_nt(a,b):
    return lax.dot_general(a.astype(BF),b.astype(BF),(((1,),(1,)),((),())),preferred_element_type=F32)
def split2(a):
    hi=a.astype(BF); lo=(a-hi.astype(F32)).astype(BF); return hi,lo
def dot3(a,b):
    ah,al=split2(a); bh,bl=split2(b)
    return bdot(ah,bh)+bdot(ah,bl)+bdot(al,bh)
def silu(x):
    return x/(1.0+jnp.exp(-x))
def softplus_of(x):
    e=jnp.exp(-jnp.abs(x)); u=1.0+e
    l=jnp.where(u==1.0,e,jnp.log(u)*e/jnp.where(u==1.0,1.0,u-1.0))
    return jnp.maximum(x,0.0)+l

def local_kernel(q_ref,k_ref,v_ref,halo_ref,qt_ref,kt_ref,vt_ref,bl_ref,dl_ref,
                 oloc_ref,qeff_ref,pair_ref,ext, *, prec=1):
    T=q_ref.shape[0]
    qc=q_ref.shape[1]; kc=k_ref.shape[1]; vc=v_ref.shape[1]
    ext[5:8,:]=halo_ref[...].astype(F32)
    ext[8:8+T,0:qc]=q_ref[...].astype(F32)
    ext[8:8+T,qc:qc+kc]=k_ref[...].astype(F32)
    ext[8:8+T,qc+kc:]=v_ref[...].astype(F32)
    def conv(lo,w_ref,wlo):
        s=w_ref[0:1,wlo:wlo+C]*ext[5:5+T,lo:lo+C]
        for j in range(1,4):
            s=s+w_ref[j:j+1,wlo:wlo+C]*ext[5+j:5+j+T,lo:lo+C]
        return silu(s)
    HKl=kc//C; HVl=vc//C; rep=HVl//HKl
    row=lax.broadcasted_iota(jnp.int32,(T,T),0); col=lax.broadcasted_iota(jnp.int32,(T,T),1)
    tri=(row>=col).astype(BF)
    beta=1.0/(1.0+jnp.exp(-bl_ref[...]))
    dec=-softplus_of(dl_ref[...])
    d1=dec.astype(BF); r=dec-d1.astype(F32); d2=r.astype(BF); d3=(r-d2.astype(F32)).astype(BF)
    lf=bdot(tri,d1)+bdot(tri,d2)+bdot(tri,d3)
    lfr=jnp.transpose(lf)
    ex=jnp.exp(lf)
    last=lf[T-1:T,:]
    tail=jnp.exp(last-lf)
    f1=jnp.exp(last)-1.0
    ri=lax.broadcasted_iota(jnp.int32,(C,C),0); ci=lax.broadcasted_iota(jnp.int32,(C,C),1)
    eye=(ri==ci).astype(F32)
    strict=ri>ci; within=ri>=ci
    sl=lambda c: slice(c*C,(c+1)*C)
    qs=[];ks=[];KK=[];QK=[];kT=[]
    for j in range(HKl):
        k=conv(qc+j*C,kt_ref,j*C)
        k=k*lax.rsqrt(jnp.sum(k*k,-1,keepdims=True)+EPS)
        q=conv(j*C,qt_ref,j*C)
        kb=k.astype(BF); qb=q.astype(BF)
        ks.append(kb); qs.append(qb)
        kT.append(jnp.transpose(k).astype(BF))
        KK.append({(c,e):bdot_nt(kb[sl(c)],kb[sl(e)]) for c in range(NC) for e in range(c+1)})
        QK.append({(c,e):bdot_nt(qb[sl(c)],kb[sl(e)]) for c in range(NC) for e in range(c+1)})
    A={};S={}
    for h in range(HVl):
        j=h//rep
        for c in range(NC):
            for e in range(c+1):
                g=jnp.exp(jnp.minimum(lf[sl(c),h:h+1]-lfr[h:h+1,sl(e)],0.0))
                s=g*QK[j][c,e]; a=(beta[sl(c),h:h+1]*g)*KK[j][c,e]
                if c==e:
                    s=jnp.where(within,s,0.0); a=jnp.where(strict,a,0.0)
                S[h,c,e]=s.astype(BF); A[h,c,e]=a
    keys=[(h,c) for h in range(HVl) for c in range(NC)]
    Tm={}
    def mask(s):
        return ((ri//(2*s))==(ci//(2*s)))&((ri//s)%2==1)&((ci//s)%2==0)
    m=mask(1)
    for key in keys:
        Tm[key]=eye-jnp.where(m,A[key+(key[1],)],0.0)
    s=2
    dd=bdot if prec==1 else dot3
    while s<C:
        m=mask(s)
        tmp={key:dd(jnp.where(m,A[key+(key[1],)],0.0),Tm[key]) for key in keys}
        Tm={key:Tm[key]-dd(Tm[key],tmp[key]) for key in keys}
        s*=2
    X={}
    for c in range(NC):
        for h in range(HVl):
            j=h//rep
            bcol=beta[sl(c),h:h+1]
            v=conv(qc+kc+h*C,vt_ref,h*C)[sl(c)] if False else None
        rhs={}
        for h in range(HVl):
            j=h//rep
            bcol=beta[sl(c),h:h+1]
            rr=ext_v(ext,vt_ref,qc+kc+h*C,h*C,c)
            R=jnp.concatenate([bcol*rr,(bcol*ex[sl(c),h:h+1])*ks[j][sl(c)].astype(F32)],1)
            for e in range(c):
                R=R-bdot(A[h,c,e],X[h,e])
            rhs[h]=R
        for h in range(HVl):
            X[h,c]=bdot(Tm[h,c],rhs[h])
    for h in range(HVl):
        j=h//rep
        for c in range(NC):
            ow=bdot(S[h,c,0],X[h,0])
            for e in range(1,c+1):
                ow=ow+bdot(S[h,c,e],X[h,e])
            oloc_ref[h,sl(c),:]=ow[:,:C]
            qeff_ref[h,sl(c),:]=(ex[sl(c),h:h+1]*qs[j][sl(c)].astype(F32)-ow[:,C:]).astype(BF)
        hw=None
        for c in range(NC):
            p=bdot(kT[j][:,sl(c)],tail[sl(c),h:h+1]*X[h,c])
            hw=p if hw is None else hw+p
        pair_ref[h,:,:C]=(f1[:,h:h+1]*eye-hw[:,C:]).astype(BF)
        pair_ref[h,:,C:]=hw[:,:C].astype(BF)
def ext_v(ext,w_ref,lo,wlo,c):
    s=w_ref[0:1,wlo:wlo+C]*ext[5+c*C:5+c*C+C,lo:lo+C]
    for j in range(1,4):
        s=s+w_ref[j:j+1,wlo:wlo+C]*ext[5+j+c*C:5+j+c*C+C,lo:lo+C]
    return silu(s)

def local_call(q,k,v,halo,qt,kt,vt,bl,dl,interpret=False,prec=1):
    T=q.shape[0]; HV=v.shape[1]//C
    return pl.pallas_call(functools.partial(local_kernel,prec=prec),
        out_shape=(jax.ShapeDtypeStruct((HV,T,C),F32),jax.ShapeDtypeStruct((HV,T,C),BF),jax.ShapeDtypeStruct((HV,C,2*C),BF)),
        scratch_shapes=[pltpu.VMEM((T+8,q.shape[1]+k.shape[1]+v.shape[1]),F32)],
        compiler_params=pltpu.CompilerParams(vmem_limit_bytes=48<<20),
        interpret=interpret)(q,k,v,halo,qt,kt,vt,bl,dl)

from jax.sharding import PartitionSpec as P
def comp(p2,p1):
    return p2+p1+jnp.einsum("hij,hjk->hik",p2[...,:C].astype(BF),p1.astype(BF),preferred_element_type=F32)
def app(p,s):
    return s+p[...,C:]+jnp.einsum("hij,hjk->hik",p[...,:C].astype(BF),s.astype(BF),preferred_element_type=F32)

def finish_kernel(oloc_ref,qeff_ref,sin_ref,gate_ref,gain_ref,w_ref,out_ref,nrm):
    for h in range(oloc_ref.shape[0]):
        o=oloc_ref[h]+bdot(qeff_ref[h],sin_ref[h])
        o=o*lax.rsqrt(jnp.mean(o*o,-1,keepdims=True)+EPS)
        o=o*gain_ref[...]*silu(gate_ref[:,h*C:(h+1)*C].astype(F32))
        nrm[:,h*C:(h+1)*C]=o.astype(BF)
    for n in range(0,w_ref.shape[1],512):
        out_ref[:,n:n+512]=bdot(nrm[...],w_ref[:,n:n+512]).astype(BF)

def shards(q,k,v,gate,qt,kt,vt,bl,dl,gain,w):
    tail=jnp.concatenate([q[-3:],k[-3:],v[-3:]],1)
    n=lax.axis_size("seq")
    halo=lax.ppermute(tail,"seq",[(i,i+1) for i in range(n-1)])
    oloc,qeff,pair=local_call(q,k,v,halo,qt,kt,vt,bl,dl)
    me=lax.axis_index("seq"); x=me//16; z=me%16
    allp=lax.all_gather(pair,"seq",axis_index_groups=[[16*i+j for j in range(16)] for i in range(4)])
    zero=jnp.zeros(pair.shape,F32)
    def one(i,c):
        acc,pre=c
        pre=jnp.where(i==z,acc,pre)
        return comp(lax.dynamic_index_in_dim(allp,i,0,False).astype(F32),acc),pre
    tot,pre=lax.fori_loop(0,16,one,(zero,zero))
    rows=lax.all_gather(tot.astype(BF),"seq",axis_index_groups=[[16*i+j for i in range(4)] for j in range(16)])
    s=jnp.zeros((pair.shape[0],C,C),F32); mine=s
    for i in range(4):
        mine=jnp.where(i==x,s,mine)
        s=app(rows[i].astype(F32),s)
    sin=app(pre,mine).astype(BF)
    part=pl.pallas_call(finish_kernel,out_shape=jax.ShapeDtypeStruct((q.shape[0],w.shape[1]),BF),
        scratch_shapes=[pltpu.VMEM((q.shape[0],w.shape[0]),BF)],
        compiler_params=pltpu.CompilerParams(vmem_limit_bytes=48<<20))(oloc,qeff,sin,gate,gain.reshape(1,C),w)
    return lax.psum_scatter(part,"head",scatter_dimension=0,tiled=True)

def solution(mesh):
    placed=(P("seq","head"),)*4+(P(None,"head"),)*3+(P("seq","head"),)*2+(P(),P("head",None))
    return jax.shard_map(shards,mesh=mesh,in_specs=placed,out_specs=P(("seq","head"),None),check_vma=False)
```

```python
import functools
import jax, jax.numpy as jnp
from jax import lax
from jax.experimental import pallas as pl
from jax.experimental.pallas import tpu as pltpu
EPS=1e-6
F32=jnp.float32; BF=jnp.bfloat16
C=128
NC=3
def bdot(a,b):
    return lax.dot_general(a.astype(BF),b.astype(BF),(((1,),(0,)),((),())),preferred_element_type=F32)
def bdot_nt(a,b):
    return lax.dot_general(a.astype(BF),b.astype(BF),(((1,),(1,)),((),())),preferred_element_type=F32)
def split2(a):
    hi=a.astype(BF); lo=(a-hi.astype(F32)).astype(BF); return hi,lo
def dot3(a,b):
    ah,al=split2(a); bh,bl=split2(b)
    return bdot(ah,bh)+bdot(ah,bl)+bdot(al,bh)
def silu(x):
    return x/(1.0+jnp.exp(-x))
def softplus_of(x):
    e=jnp.exp(-jnp.abs(x)); u=1.0+e
    l=jnp.where(u==1.0,e,jnp.log(u)*e/jnp.where(u==1.0,1.0,u-1.0))
    return jnp.maximum(x,0.0)+l

def local_kernel(q_ref,k_ref,v_ref,halo_ref,qt_ref,kt_ref,vt_ref,bl_ref,dl_ref,
                 oloc_ref,qeff_ref,pair_ref,ext, *, prec=1):
    T=q_ref.shape[0]
    qc=q_ref.shape[1]; kc=k_ref.shape[1]; vc=v_ref.shape[1]
    ext[5:8,:]=halo_ref[...].astype(F32)
    ext[8:8+T,0:qc]=q_ref[...].astype(F32)
    ext[8:8+T,qc:qc+kc]=k_ref[...].astype(F32)
    ext[8:8+T,qc+kc:]=v_ref[...].astype(F32)
    def conv(lo,w_ref,wlo):
        s=w_ref[0:1,wlo:wlo+C]*ext[5:5+T,lo:lo+C]
        for j in range(1,4):
            s=s+w_ref[j:j+1,wlo:wlo+C]*ext[5+j:5+j+T,lo:lo+C]
        return silu(s)
    HKl=kc//C; HVl=vc//C; rep=HVl//HKl
    row=lax.broadcasted_iota(jnp.int32,(T,T),0); col=lax.broadcasted_iota(jnp.int32,(T,T),1)
    tri=(row>=col).astype(BF)
    beta=1.0/(1.0+jnp.exp(-bl_ref[...]))
    dec=-softplus_of(dl_ref[...])
    d1=dec.astype(BF); r=dec-d1.astype(F32); d2=r.astype(BF); d3=(r-d2.astype(F32)).astype(BF)
    lf=bdot(tri,d1)+bdot(tri,d2)+bdot(tri,d3)
    lfr=jnp.transpose(lf)
    ex=jnp.exp(lf)
    last=lf[T-1:T,:]
    tail=jnp.exp(last-lf)
    f1=jnp.exp(last)-1.0
    ri=lax.broadcasted_iota(jnp.int32,(C,C),0); ci=lax.broadcasted_iota(jnp.int32,(C,C),1)
    eye=(ri==ci).astype(F32)
    strict=ri>ci; within=ri>=ci
    sl=lambda c: slice(c*C,(c+1)*C)
    qs=[];ks=[];KK=[];QK=[];kT=[]
    for j in range(HKl):
        k=conv(qc+j*C,kt_ref,j*C)
        k=k*lax.rsqrt(jnp.sum(k*k,-1,keepdims=True)+EPS)
        q=conv(j*C,qt_ref,j*C)
        kb=k.astype(BF); qb=q.astype(BF)
        ks.append(kb); qs.append(qb)
        kT.append(jnp.transpose(k).astype(BF))
        KK.append({(c,e):bdot_nt(kb[sl(c)],kb[sl(e)]) for c in range(NC) for e in range(c+1)})
        QK.append({(c,e):bdot_nt(qb[sl(c)],kb[sl(e)]) for c in range(NC) for e in range(c+1)})
    A={};S={}
    for h in range(HVl):
        j=h//rep
        for c in range(NC):
            for e in range(c+1):
                g=jnp.exp(jnp.minimum(lf[sl(c),h:h+1]-lfr[h:h+1,sl(e)],0.0))
                s=g*QK[j][c,e]; a=(beta[sl(c),h:h+1]*g)*KK[j][c,e]
                if c==e:
                    s=jnp.where(within,s,0.0); a=jnp.where(strict,a,0.0)
                S[h,c,e]=s.astype(BF); A[h,c,e]=a
    keys=[(h,c) for h in range(HVl) for c in range(NC)]
    Tm={}
    def mask(s):
        return ((ri//(2*s))==(ci//(2*s)))&((ri//s)%2==1)&((ci//s)%2==0)
    m=mask(1)
    for key in keys:
        Tm[key]=eye-jnp.where(m,A[key+(key[1],)],0.0)
    s=2
    dd=bdot if prec==1 else dot3
    while s<C:
        m=mask(s)
        tmp={key:dd(jnp.where(m,A[key+(key[1],)],0.0),Tm[key]) for key in keys}
        Tm={key:Tm[key]-dd(Tm[key],tmp[key]) for key in keys}
        s*=2
    X={}
    for c in range(NC):
        for h in range(HVl):
            j=h//rep
            bcol=beta[sl(c),h:h+1]
            v=conv(qc+kc+h*C,vt_ref,h*C)[sl(c)] if False else None
        rhs={}
        for h in range(HVl):
            j=h//rep
            bcol=beta[sl(c),h:h+1]
            rr=ext_v(ext,vt_ref,qc+kc+h*C,h*C,c)
            R=jnp.concatenate([bcol*rr,(bcol*ex[sl(c),h:h+1])*ks[j][sl(c)].astype(F32)],1)
            for e in range(c):
                R=R-bdot(A[h,c,e],X[h,e])
            rhs[h]=R
        for h in range(HVl):
            X[h,c]=bdot(Tm[h,c],rhs[h])
    for h in range(HVl):
        j=h//rep
        for c in range(NC):
            ow=bdot(S[h,c,0],X[h,0])
            for e in range(1,c+1):
                ow=ow+bdot(S[h,c,e],X[h,e])
            oloc_ref[h,sl(c),:]=ow[:,:C]
            qeff_ref[h,sl(c),:]=(ex[sl(c),h:h+1]*qs[j][sl(c)].astype(F32)-ow[:,C:]).astype(BF)
        hw=None
        for c in range(NC):
            p=bdot(kT[j][:,sl(c)],tail[sl(c),h:h+1]*X[h,c])
            hw=p if hw is None else hw+p
        pair_ref[h,:,:C]=(f1[:,h:h+1]*eye-hw[:,C:]).astype(BF)
        pair_ref[h,:,C:]=hw[:,:C].astype(BF)
def ext_v(ext,w_ref,lo,wlo,c):
    s=w_ref[0:1,wlo:wlo+C]*ext[5+c*C:5+c*C+C,lo:lo+C]
    for j in range(1,4):
        s=s+w_ref[j:j+1,wlo:wlo+C]*ext[5+j+c*C:5+j+c*C+C,lo:lo+C]
    return silu(s)

def local_call(q,k,v,halo,qt,kt,vt,bl,dl,interpret=False,prec=1):
    T=q.shape[0]; HV=v.shape[1]//C
    return pl.pallas_call(functools.partial(local_kernel,prec=prec),
        out_shape=(jax.ShapeDtypeStruct((HV,T,C),F32),jax.ShapeDtypeStruct((HV,T,C),BF),jax.ShapeDtypeStruct((HV,C,2*C),BF)),
        scratch_shapes=[pltpu.VMEM((T+8,q.shape[1]+k.shape[1]+v.shape[1]),F32)],
        compiler_params=pltpu.CompilerParams(vmem_limit_bytes=60<<20),
        interpret=interpret)(q,k,v,halo,qt,kt,vt,bl,dl)

from jax.sharding import PartitionSpec as P
MESH=pl.DeviceIdType.MESH
NL=4
NG=4
NX=4
NY=4
CH=4

def compose(later,earlier):
    return later+earlier+bdot(later[:,:C],earlier)

def exchange(axis,me_slot,device_of,src_of,land,send,recv):
    copies=[]
    for off in range(1,4):
        slot=lax.rem(me_slot+off,4)
        cp=pltpu.make_async_remote_copy(src_ref=src_of(slot),dst_ref=land.at[me_slot],send_sem=send.at[off-1],
            recv_sem=recv.at[me_slot],device_id={axis:device_of(slot)},device_id_type=MESH)
        cp.start()
        copies.append(cp)
    def finish():
        for off in range(1,4):
            slot=lax.rem(me_slot+off,4)
            pltpu.make_async_remote_copy(src_ref=src_of(slot),dst_ref=land.at[slot],send_sem=send.at[off-1],
                recv_sem=recv.at[slot],device_id={axis:device_of(slot)},device_id_type=MESH).wait_recv()
    return copies,finish

def scan_body(pair,sin,buf1,pre,tot,buf2,gpre,rowt,buf3,rpre,outb,s1,r1,s2,r2,s3,r3,s4,r4):
    me=lax.axis_index("seq")
    l=lax.rem(me,NL); g=lax.rem(me//NL,NG); x=me//(NL*NG)
    dl=lambda i: me-l+i
    dg=lambda i: me+(i-g)*NL
    dx=lambda i: me+(i-x)*(NL*NG)
    c1,w1=exchange("seq",l,dl,lambda i: pair.at[i],buf1,s1,r1)
    buf1[l]=pair[l]
    w1()
    acc=buf1[0].astype(F32)
    pre[0]=jnp.zeros((C,2*C),F32)
    for i in range(1,NL):
        pre[i]=acc
        acc=compose(buf1[i].astype(F32),acc)
    tot[...]=acc.astype(BF)
    c2,w2=exchange("seq",g,dg,lambda i: tot,buf2,s2,r2)
    buf2[g]=tot[...]
    w2()
    acc=buf2[0].astype(F32)
    gpre[0]=jnp.zeros((C,2*C),F32)
    for i in range(1,NG):
        gpre[i]=acc
        acc=compose(buf2[i].astype(F32),acc)
    rowt[...]=acc.astype(BF)
    c3,w3=exchange("seq",x,dx,lambda i: rowt,buf3,s3,r3)
    buf3[x]=rowt[...]
    w3()
    s=buf3[0,:,C:].astype(F32)
    rpre[0]=jnp.zeros((C,C),F32)
    for i in range(1,NX):
        rpre[i]=s
        s=s+buf3[i,:,C:].astype(F32)+bdot(buf3[i,:,:C],s)
    row_in=rpre[x]
    gp=gpre[g]
    grp=row_in+gp[:,C:]+bdot(gp[:,:C],row_in)
    for i in range(NL):
        p=pre[i]
        outb[i]=(grp+p[:,C:]+bdot(p[:,:C],grp)).astype(BF)
    c4,w4=exchange("seq",l,dl,lambda i: outb.at[i],sin,s4,r4)
    sin[l]=outb[l]
    w4()
    for cp in c1+c2+c3+c4:
        cp.wait_send()

def scan_peers():
    me=lax.axis_index("seq")
    l=lax.rem(me,NL); g=lax.rem(me//NL,NG); x=me//(NL*NG)
    out=[]
    for off in range(1,4):
        out.append(me-l+lax.rem(l+off,4))
        out.append(me+(lax.rem(g+off,4)-g)*NL)
        out.append(me+(lax.rem(x+off,4)-x)*(NL*NG))
    return out

def scan_kernel(pair,out,sin,*rest):
    barrier=pltpu.get_barrier_semaphore()
    for d in scan_peers():
        pl.semaphore_signal(barrier,inc=1,device_id={"seq":d},device_id_type=MESH)
    pl.semaphore_wait(barrier,9)
    scan_body(pair,sin,*rest)
    out[...]=sin[...]

def scan_scratch():
    D=pltpu.SemaphoreType.DMA
    return [pltpu.VMEM((4,C,C),BF),pltpu.VMEM((4,C,2*C),BF),pltpu.VMEM((4,C,2*C),F32),pltpu.VMEM((C,2*C),BF),
        pltpu.VMEM((4,C,2*C),BF),pltpu.VMEM((4,C,2*C),F32),pltpu.VMEM((C,2*C),BF),pltpu.VMEM((4,C,2*C),BF),
        pltpu.VMEM((4,C,C),F32),pltpu.VMEM((4,C,C),BF)]+[D((3,)),D((4,))]*4

def scan_call(pair):
    return pl.pallas_call(scan_kernel,out_shape=jax.ShapeDtypeStruct((4,C,C),BF),scratch_shapes=scan_scratch(),
        compiler_params=pltpu.CompilerParams(collective_id=1,has_side_effects=True,vmem_limit_bytes=60<<20))(pair)

def finish_body(oloc,qeff,sin,gate,gain,w,out,nrm,part,land,pair_sum,gath,sa,ra,sb,rb):
    hd=lax.axis_index("head"); y=hd//2; c=lax.rem(hd,2)
    for h in range(4):
        o=oloc[h]+bdot(qeff[h],sin[h])
        o=o*lax.rsqrt(jnp.mean(o*o,-1,keepdims=True)+EPS)
        o=o*gain[...]*silu(gate[:,h*C:(h+1)*C].astype(F32))
        nrm[:,h*C:(h+1)*C]=o.astype(BF)
    wide=w.shape[1]//CH
    rows=nrm.shape[0]//8
    def first(n):
        return pltpu.make_async_remote_copy(src_ref=part.at[n,1-c],dst_ref=land.at[n],send_sem=sa.at[n],recv_sem=ra.at[n],
            device_id={"head":hd+1-2*c},device_id_type=MESH)
    for n in range(CH):
        p=bdot(nrm[...],w[:,n*wide:(n+1)*wide]).astype(BF)
        for b in range(8):
            part[n,b%2,b//2]=p[b*rows:(b+1)*rows]
        first(n).start()
    def second(n,off,slot):
        to=lax.rem(y+off,NY)
        return pltpu.make_async_remote_copy(src_ref=pair_sum.at[n,to],dst_ref=gath.at[n,slot],send_sem=sb.at[n,off-1],
            recv_sem=rb.at[n,slot],device_id={"head":2*to+c},device_id_type=MESH)
    for n in range(CH):
        first(n).wait_recv()
        pair_sum[n]=(part[n,c].astype(F32)+land[n].astype(F32)).astype(BF)
        for off in range(1,4):
            second(n,off,y).start()
        gath[n,y]=pair_sum[n,y]
    for n in range(CH):
        for off in range(1,4):
            second(n,off,lax.rem(y+off,NY)).wait_recv()
        t=gath[n,0].astype(F32)
        for i in range(1,NY):
            t=t+gath[n,i].astype(F32)
        out[:,n*wide:(n+1)*wide]=t.astype(BF)
    for n in range(CH):
        first(n).wait_send()
        for off in range(1,4):
            second(n,off,y).wait_send()

def finish_peers():
    hd=lax.axis_index("head"); y=hd//2; c=lax.rem(hd,2)
    return [hd+1-2*c]+[2*lax.rem(y+off,NY)+c for off in range(1,4)]

def finish_kernel(*refs):
    barrier=pltpu.get_barrier_semaphore()
    for d in finish_peers():
        pl.semaphore_signal(barrier,inc=1,device_id={"head":d},device_id_type=MESH)
    pl.semaphore_wait(barrier,4)
    finish_body(*refs)

def finish_scratch(T,K,N):
    D=pltpu.SemaphoreType.DMA
    r=T//8; wide=N//CH
    return [pltpu.VMEM((T,K),BF),pltpu.VMEM((CH,2,4,r,wide),BF),pltpu.VMEM((CH,4,r,wide),BF),pltpu.VMEM((CH,4,r,wide),BF),
        pltpu.VMEM((CH,4,r,wide),BF),D((CH,)),D((CH,)),D((CH,3)),D((CH,4))]

def finish_call(oloc,qeff,sin,gate,gain,w):
    T=gate.shape[0]
    return pl.pallas_call(finish_kernel,out_shape=jax.ShapeDtypeStruct((T//8,w.shape[1]),BF),
        scratch_shapes=finish_scratch(T,w.shape[0],w.shape[1]),
        compiler_params=pltpu.CompilerParams(collective_id=2,has_side_effects=True,vmem_limit_bytes=60<<20))(oloc,qeff,sin,gate,gain,w)

def shards(q,k,v,gate,qt,kt,vt,bl,dl,gain,w):
    tail=jnp.concatenate([q[-3:],k[-3:],v[-3:]],1)
    n=lax.axis_size("seq")
    halo=lax.ppermute(tail,"seq",[(i,i+1) for i in range(n-1)])
    oloc,qeff,pair=local_call(q,k,v,halo,qt,kt,vt,bl,dl)
    sin=scan_call(pair)
    return finish_call(oloc,qeff,sin,gate,gain.reshape(1,C),w)

def solution(mesh):
    placed=(P("seq","head"),)*4+(P(None,"head"),)*3+(P("seq","head"),)*2+(P(),P("head",None))
    return jax.shard_map(shards,mesh=mesh,in_specs=placed,out_specs=P(("seq","head"),None),check_vma=False)
```

```python
import jax
import jax.numpy as jnp
from jax import lax
from jax.experimental import pallas as pl
from jax.experimental.pallas import tpu as pltpu
from jax.sharding import PartitionSpec as P

EPS = 1e-6
F32 = jnp.float32
BF = jnp.bfloat16
MESH = pl.DeviceIdType.MESH
C = 128
NL = 4
NG = 4
NX = 4
NY = 4
CH = 4
HALO = 16


def bdot(a, b):
    return lax.dot_general(
        a.astype(BF), b.astype(BF), (((1,), (0,)), ((), ())), preferred_element_type=F32
    )


def bdot_nt(a, b):
    return lax.dot_general(
        a.astype(BF), b.astype(BF), (((1,), (1,)), ((), ())), preferred_element_type=F32
    )


def silu(x):
    return x / (1.0 + jnp.exp(-x))


def softplus(x):
    e = jnp.exp(-jnp.abs(x))
    u = 1.0 + e
    log1p = jnp.where(u == 1.0, e, jnp.log(u) * e / jnp.where(u == 1.0, 1.0, u - 1.0))
    return jnp.maximum(x, 0.0) + log1p


def compose(later, earlier):
    return later + earlier + bdot(later[:, :C], earlier)


def applied(pair, state):
    return state + pair[:, C:] + bdot(pair[:, :C], state)


def place():
    me = lax.axis_index("seq")
    return me, lax.rem(me, NL), lax.rem(me // NL, NG), me // (NL * NG)


def signal_all(devices):
    barrier = pltpu.get_barrier_semaphore()
    for d in devices:
        pl.semaphore_signal(barrier, inc=1, device_id=d, device_id_type=MESH)


def wait_all(count):
    pl.semaphore_wait(pltpu.get_barrier_semaphore(), count)


def halo_kernel(q, k, v, out, land, send, recv):
    me = lax.axis_index("seq")
    n = lax.axis_size("seq")
    after = {"seq": lax.rem(me + 1, n)}
    before = {"seq": lax.rem(me + n - 1, n)}
    signal_all([after, before])
    wait_all(2)
    copies = []
    lo = 0
    for i, ref in enumerate((q, k, v)):
        t, w = ref.shape
        copies.append(
            pltpu.make_async_remote_copy(
                src_ref=ref.at[pl.ds(t - HALO, HALO)],
                dst_ref=land.at[:, pl.ds(lo, w)],
                send_sem=send.at[i],
                recv_sem=recv.at[i],
                device_id=after,
                device_id_type=MESH,
            )
        )
        copies[-1].start()
        lo += w
    for copy in copies:
        copy.wait()
    out[...] = jnp.where(me > 0, land[...], jnp.zeros_like(land))


def exchange(slot, device_of, src_of, land, send, recv):
    def copy(off, at):
        to = lax.rem(slot + off, 4)
        return pltpu.make_async_remote_copy(
            src_ref=src_of(to),
            dst_ref=land.at[at(to)],
            send_sem=send.at[off - 1],
            recv_sem=recv.at[at(to)],
            device_id={"seq": device_of(to)},
            device_id_type=MESH,
        )

    out = [copy(off, lambda to: slot) for off in range(1, 4)]
    for c in out:
        c.start()
    return out, [copy(off, lambda to: to) for off in range(1, 4)]


def layer_kernel(
    halo, q, k, v, gate, qt, kt, vt, blt, dlt, gain, w,
    out,
    halo_v, q_v, k_v, v_v, gate_v, qt_v, kt_v, vt_v, bl_v, dl_v, gain_v, w_v, in_sem,
    ext, cols_s, oloc, qeff, pair, gs,
    buf1, tot, buf2, rowt, buf3, outb, sin,
    s1, r1, s2, r2, s3, r3, s4, r4,
    nrm, part, land, psum, relay, final_s, from_lo, from_hi,
    sa, ra, sr, rr, sd, rd, sf, rf,
):
    pairs_in = (
        (dlt, dl_v), (blt, bl_v), (halo, halo_v), (kt, kt_v), (k, k_v), (vt, vt_v), (v, v_v),
        (qt, qt_v), (q, q_v), (gate, gate_v), (gain, gain_v), (w, w_v),
    )
    loads = {}
    for i, (src, dst) in enumerate(pairs_in):
        loads[i] = pltpu.make_async_copy(src, dst, in_sem.at[i])
        loads[i].start()
    me, l, g, x = place()
    hd = lax.axis_index("head")
    y, core = hd // 2, lax.rem(hd, 2)
    at_l = lambda i: me - l + i
    at_g = lambda i: me + (i - g) * NL
    at_x = lambda i: me + (i - x) * (NL * NG)
    sibling = {"head": hd + 1 - 2 * core}
    up = {"head": 2 * lax.rem(y + 1, NY) + core}
    down = {"head": 2 * lax.rem(y + NY - 1, NY) + core}
    peers = [sibling, up, down]
    for off in range(1, 4):
        peers.append({"seq": at_g(lax.rem(g + off, NG))})
        peers.append({"seq": at_l(lax.rem(l + off, NL))})
        peers.append({"seq": at_x(lax.rem(x + off, NX))})
    signal_all(peers)

    T = k.shape[0]
    nc = T // C
    qc, kc, vc = q.shape[1], k.shape[1], v.shape[1]
    nk, nv = kc // C, vc // C
    rep = nv // nk
    sl = lambda c: slice(c * C, (c + 1) * C)

    loads[0].wait()
    loads[1].wait()
    row = lax.broadcasted_iota(jnp.int32, (T, T), 0)
    col = lax.broadcasted_iota(jnp.int32, (T, T), 1)
    upto = (row <= col).astype(BF)
    dec = -softplus(dl_v[...])
    d1 = dec.astype(BF)
    r = dec - d1.astype(F32)
    d2 = r.astype(BF)
    d3 = (r - d2.astype(F32)).astype(BF)
    lfr = bdot(d1, upto) + bdot(d2, upto) + bdot(d3, upto)
    last = lfr[:, T - 1 : T]
    cols_s[0:4, :] = 1.0 / (1.0 + jnp.exp(-bl_v[...]))
    cols_s[4:8, :] = lfr
    cols_s[8:12, :] = jnp.exp(lfr)
    cols_s[12:16, :] = jnp.exp(last - lfr)
    cols = jnp.transpose(cols_s[...])
    beta = lambda h, c: cols[sl(c), h : h + 1]
    lf = lambda h, c: cols[sl(c), 4 + h : 5 + h]
    ex = lambda h, c: cols[sl(c), 8 + h : 9 + h]
    tail = lambda h, c: cols[sl(c), 12 + h : 13 + h]
    f1 = jnp.exp(last) - 1.0

    ri = lax.broadcasted_iota(jnp.int32, (C, C), 0)
    ci = lax.broadcasted_iota(jnp.int32, (C, C), 1)
    eye = (ri == ci).astype(F32)
    strict = ri > ci
    within = ri >= ci

    def put(lo, raw):
        wide = raw.shape[1]
        ext[5:8, lo : lo + wide] = halo_v[HALO - 3 : HALO, lo : lo + wide].astype(F32)
        ext[8 : 8 + T, lo : lo + wide] = raw[...].astype(F32)

    def conv(lo, taps, at):
        s = taps[0:1, at : at + C] * ext[5 : 5 + T, lo : lo + C]
        for j in range(1, 4):
            s = s + taps[j : j + 1, at : at + C] * ext[5 + j : 5 + j + T, lo : lo + C]
        return silu(s)

    loads[2].wait()
    loads[3].wait()
    loads[4].wait()
    put(qc, k_v)
    ks, KK, kT = [], [], []
    for j in range(nk):
        kj = conv(qc + j * C, kt_v, j * C)
        kj = kj * lax.rsqrt(jnp.sum(kj * kj, -1, keepdims=True) + EPS)
        kb = kj.astype(BF)
        ks.append(kb)
        kT.append(jnp.transpose(kj).astype(BF))
        KK.append({(c, e): bdot_nt(kb[sl(c)], kb[sl(e)]) for c in range(nc) for e in range(c + 1)})
    G = {}
    A = {}
    for h in range(nv):
        for c in range(nc):
            for e in range(c + 1):
                gap = jnp.exp(jnp.minimum(lf(h, c) - lfr[h : h + 1, sl(e)], 0.0))
                G[h, c, e] = gap
                a = (beta(h, c) * gap) * KK[h // rep][c, e]
                A[h, c, e] = jnp.where(strict, a, 0.0) if c == e else a

    keys = [(h, c) for h in range(nv) for c in range(nc)]

    def corner(s):
        return ((ri // (2 * s)) == (ci // (2 * s))) & ((ri // s) % 2 == 1) & ((ci // s) % 2 == 0)

    m = corner(1)
    inv = {(h, c): eye - jnp.where(m, A[h, c, c], 0.0) for h, c in keys}
    s = 2
    while s < C:
        m = corner(s)
        half = {(h, c): bdot(jnp.where(m, A[h, c, c], 0.0), inv[h, c]) for h, c in keys}
        inv = {key: inv[key] - bdot(inv[key], half[key]) for key in keys}
        s *= 2

    loads[5].wait()
    loads[6].wait()
    put(qc + kc, v_v)
    X = {}
    vs = [conv(qc + kc + h * C, vt_v, h * C) for h in range(nv)]
    for c in range(nc):
        rhs = {}
        for h in range(nv):
            kf = ks[h // rep][sl(c)].astype(F32)
            R = jnp.concatenate([beta(h, c) * vs[h][sl(c)], (beta(h, c) * ex(h, c)) * kf], 1)
            for e in range(c):
                R = R - bdot(A[h, c, e], X[h, e])
            rhs[h] = R
        for h in range(nv):
            X[h, c] = bdot(inv[h, c], rhs[h])
    for h in range(nv):
        hw = bdot(kT[h // rep][:, sl(0)], tail(h, 0) * X[h, 0])
        for c in range(1, nc):
            hw = hw + bdot(kT[h // rep][:, sl(c)], tail(h, c) * X[h, c])
        pair[h, :, :C] = (f1[h : h + 1, :] * eye - hw[:, C:]).astype(BF)
        pair[h, :, C:] = hw[:, :C].astype(BF)

    wait_all(len(peers))
    c1, w1 = exchange(l, at_l, lambda i: pair.at[i], buf1, s1, r1)
    buf1[l] = pair[l]

    loads[7].wait()
    loads[8].wait()
    put(0, q_v)
    for j in range(nk):
        qj = conv(j * C, qt_v, j * C)
        qb = qj.astype(BF)
        for c in range(nc):
            QK = {e: bdot_nt(qb[sl(c)], ks[j][sl(e)]) for e in range(c + 1)}
            for h in range(j * rep, (j + 1) * rep):
                ow = None
                for e in range(c + 1):
                    sc = G[h, c, e] * QK[e]
                    if c == e:
                        sc = jnp.where(within, sc, 0.0)
                    p = bdot(sc, X[h, e])
                    ow = p if ow is None else ow + p
                oloc[h, sl(c), :] = ow[:, :C]
                qeff[h, sl(c), :] = (ex(h, c) * qj[sl(c)] - ow[:, C:]).astype(BF)

    for copy in w1:
        copy.wait_recv()
    e0, e1, e2, e3 = [buf1[i].astype(F32) for i in range(NL)]
    p2 = compose(e1, e0)
    tot[...] = compose(compose(e3, e2), p2).astype(BF)
    c2, w2 = exchange(g, at_g, lambda i: tot, buf2, s2, r2)
    buf2[g] = tot[...]
    p3 = compose(e2, p2)

    loads[9].wait()
    loads[10].wait()
    for h in range(nv):
        gs[:, sl(h)] = gain_v[...] * silu(gate_v[:, sl(h)].astype(F32))

    for copy in w2:
        copy.wait_recv()
    g0, g1, g2, g3 = [buf2[i].astype(F32) for i in range(NG)]
    q2 = compose(g1, g0)
    rowt[...] = compose(compose(g3, g2), q2).astype(BF)
    c3, w3 = exchange(x, at_x, lambda i: rowt, buf3, s3, r3)
    buf3[x] = rowt[...]
    q3 = compose(g2, q2)
    zero = jnp.zeros((C, 2 * C), F32)
    gp = jnp.where(g == 0, zero, jnp.where(g == 1, g0, jnp.where(g == 2, q2, q3)))
    full = [gp] + [compose(p, gp) for p in (e0, p2, p3)]

    for copy in w3:
        copy.wait_recv()
    state1 = buf3[0, :, C:].astype(F32)
    state2 = applied(buf3[1].astype(F32), state1)
    state3 = applied(buf3[2].astype(F32), state2)
    row_in = jnp.where(
        x == 0, zero[:, :C], jnp.where(x == 1, state1, jnp.where(x == 2, state2, state3))
    )
    for i in range(NL):
        outb[i] = applied(full[i], row_in).astype(BF)
    c4, w4 = exchange(l, at_l, lambda i: outb.at[i], sin, s4, r4)
    sin[l] = outb[l]
    loads[11].wait()
    for copy in w4:
        copy.wait_recv()

    for h in range(nv):
        o = oloc[h] + bdot(qeff[h], sin[h])
        o = o * lax.rsqrt(jnp.mean(o * o, -1, keepdims=True) + EPS)
        nrm[:, sl(h)] = (o * gs[:, sl(h)]).astype(BF)

    wide = w.shape[1] // CH
    rows = T // 8

    def remote(src, dst, send, recv, device):
        return pltpu.make_async_remote_copy(
            src_ref=src, dst_ref=dst, send_sem=send, recv_sem=recv,
            device_id=device, device_id_type=MESH,
        )

    y_up, y_down, y_far = lax.rem(y + 1, NY), lax.rem(y + NY - 1, NY), lax.rem(y + 2, NY)
    within_chip = [
        remote(part.at[n, 1 - core], land.at[n], sa.at[n], ra.at[n], sibling) for n in range(CH)
    ]
    for n in range(CH):
        p = bdot(nrm[...], w_v[:, n * wide : (n + 1) * wide]).astype(BF)
        for b in range(8):
            part[n, b % 2, b // 2] = p[b * rows : (b + 1) * rows]
        within_chip[n].start()
    far, direct, last_hop = [], [], []
    for n in range(CH):
        a_dev, b_dev = (up, down) if n % 2 == 0 else (down, up)
        a_y, b_y = (y_up, y_down) if n % 2 == 0 else (y_down, y_up)
        a_land, b_land = (from_lo, from_hi) if n % 2 == 0 else (from_hi, from_lo)
        far.append(remote(psum.at[n, y_far], relay.at[n], sr.at[n], rr.at[n], a_dev))
        direct.append(remote(psum.at[n, b_y], b_land.at[n], sd.at[n], rd.at[n], b_dev))
        last_hop.append(remote(final_s.at[n], a_land.at[n], sf.at[n], rf.at[n], a_dev))
    for n in range(CH):
        within_chip[n].wait_recv()
        psum[n] = (part[n, core].astype(F32) + land[n].astype(F32)).astype(BF)
        far[n].start()
        direct[n].start()
    for n in range(CH):
        a_y = y_up if n % 2 == 0 else y_down
        far[n].wait_recv()
        final_s[n] = (psum[n, a_y].astype(F32) + relay[n].astype(F32)).astype(BF)
        last_hop[n].start()
    for n in range(CH):
        direct[n].wait_recv()
        last_hop[n].wait_recv()
        t = psum[n, y].astype(F32) + from_lo[n].astype(F32) + from_hi[n].astype(F32)
        out[:, n * wide : (n + 1) * wide] = t.astype(BF)
    for copy in c1 + c2 + c3 + c4 + within_chip + far + direct + last_hop:
        copy.wait_send()


def shards(q, k, v, gate, qt, kt, vt, bl, dl, gain, w):
    D = pltpu.SemaphoreType.DMA
    V = pltpu.VMEM
    any_space = pl.BlockSpec(memory_space=pl.ANY)
    vmem = pl.BlockSpec(memory_space=pltpu.VMEM)
    T = q.shape[0]
    wide_in = q.shape[1] + k.shape[1] + v.shape[1]
    halo = pl.pallas_call(
        halo_kernel,
        out_shape=jax.ShapeDtypeStruct((HALO, wide_in), BF),
        in_specs=[any_space] * 3,
        out_specs=vmem,
        scratch_shapes=[V((HALO, wide_in), BF), D((3,)), D((3,))],
        compiler_params=pltpu.CompilerParams(
            collective_id=1, has_side_effects=True, vmem_limit_bytes=60 << 20
        ),
        name="halo",
    )(q, k, v)
    args = (halo, q, k, v, gate, qt, kt, vt, bl.T, dl.T, gain.reshape(1, C), w)
    nv = v.shape[1] // C
    r, wide = T // 8, w.shape[1] // CH
    chunk = V((CH, r, wide), BF)
    four = V((CH, NY, r, wide), BF)
    scratch = [V(a.shape, a.dtype) for a in args]
    scratch += [D((len(args),))]
    scratch += [
        V((T + 8, wide_in), F32), V((16, T), F32), V((nv, T, C), F32), V((nv, T, C), BF),
        V((nv, C, 2 * C), BF), V((T, nv * C), F32),
    ]
    slots = V((4, C, 2 * C), BF)
    scratch += [slots, V((C, 2 * C), BF), slots, V((C, 2 * C), BF), slots]
    scratch += [V((4, C, C), BF), V((4, C, C), BF)]
    scratch += [D((3,)), D((4,))] * 4
    scratch += [V((T, nv * C), BF), V((CH, 2, NY, r, wide), BF), four, four]
    scratch += [chunk] * 4 + [D((CH,))] * 8
    return pl.pallas_call(
        layer_kernel,
        out_shape=jax.ShapeDtypeStruct((r, w.shape[1]), BF),
        in_specs=[any_space] * len(args),
        out_specs=vmem,
        scratch_shapes=scratch,
        compiler_params=pltpu.CompilerParams(
            collective_id=2, has_side_effects=True, vmem_limit_bytes=60 << 20
        ),
        name="layer",
    )(*args)


def solution(mesh):
    tokens_heads = P("seq", "head")
    placed = (tokens_heads,) * 4 + (P(None, "head"),) * 3 + (tokens_heads,) * 2
    return jax.shard_map(
        shards,
        mesh=mesh,
        in_specs=placed + (P(), P("head", None)),
        out_specs=P(("seq", "head"), None),
        check_vma=False,
    )
```

```python
import jax
import jax.numpy as jnp
from jax import lax
from jax.experimental import pallas as pl
from jax.experimental.pallas import tpu as pltpu
from jax.sharding import PartitionSpec as P

EPS = 1e-6
F32 = jnp.float32
BF = jnp.bfloat16
MESH = pl.DeviceIdType.MESH
C = 128
NL = 4
NG = 4
NX = 4
NY = 4
CH = 4
HALO = 16


def bdot(a, b):
    return lax.dot_general(
        a.astype(BF), b.astype(BF), (((1,), (0,)), ((), ())), preferred_element_type=F32
    )


def bdot_nt(a, b):
    return lax.dot_general(
        a.astype(BF), b.astype(BF), (((1,), (1,)), ((), ())), preferred_element_type=F32
    )


def silu(x):
    return x / (1.0 + jnp.exp(-x))


def softplus(x):
    e = jnp.exp(-jnp.abs(x))
    u = 1.0 + e
    log1p = jnp.where(u == 1.0, e, jnp.log(u) * e / jnp.where(u == 1.0, 1.0, u - 1.0))
    return jnp.maximum(x, 0.0) + log1p


def compose(later, earlier):
    return later + earlier + bdot(later[:, :C], earlier)


def applied(pair, state):
    return state + pair[:, C:] + bdot(pair[:, :C], state)


def place():
    me = lax.axis_index("seq")
    return me, lax.rem(me, NL), lax.rem(me // NL, NG), me // (NL * NG)


def signal_all(devices):
    barrier = pltpu.get_barrier_semaphore()
    for d in devices:
        pl.semaphore_signal(barrier, inc=1, device_id=d, device_id_type=MESH)


def wait_all(count):
    pl.semaphore_wait(pltpu.get_barrier_semaphore(), count)


def exchange(slot, device_of, src_of, land, send, recv):
    def copy(off, at):
        to = lax.rem(slot + off, 4)
        return pltpu.make_async_remote_copy(
            src_ref=src_of(to),
            dst_ref=land.at[at(to)],
            send_sem=send.at[off - 1],
            recv_sem=recv.at[at(to)],
            device_id={"seq": device_of(to)},
            device_id_type=MESH,
        )

    out = [copy(off, lambda to: slot) for off in range(1, 4)]
    for c in out:
        c.start()
    return out, [copy(off, lambda to: to) for off in range(1, 4)]


def layer_kernel(
    q, k, v, gate, qt, kt, vt, blt, dlt, gain, w,
    out,
    q_v, k_v, v_v, gate_v, qt_v, kt_v, vt_v, bl_v, dl_v, gain_v, w_v, in_sem,
    halo_v, w_sib, sh, rh, sw, rw,
    ext, cols_s, oloc, qeff, pair, gs,
    buf1, tot, buf2, rowt, buf3, outb, sin,
    s1, r1, s2, r2, s3, r3, s4, r4,
    nrm, n_sib, acc, psum, relay, final_s, from_lo, from_hi,
    sa, ra, sr, rr, sd, rd, sf, rf,
):
    pairs_in = (
        (dlt, dl_v), (blt, bl_v), (kt, kt_v), (k, k_v), (vt, vt_v), (v, v_v),
        (qt, qt_v), (q, q_v), (gate, gate_v), (gain, gain_v), (w, w_v),
    )
    loads = {}
    for i, (src, dst) in enumerate(pairs_in):
        loads[i] = pltpu.make_async_copy(src, dst, in_sem.at[i])
        loads[i].start()
    me, l, g, x = place()
    hd = lax.axis_index("head")
    y, core = hd // 2, lax.rem(hd, 2)
    at_l = lambda i: me - l + i
    at_g = lambda i: me + (i - g) * NL
    at_x = lambda i: me + (i - x) * (NL * NG)
    sibling = {"head": hd + 1 - 2 * core}
    up = {"head": 2 * lax.rem(y + 1, NY) + core}
    down = {"head": 2 * lax.rem(y + NY - 1, NY) + core}
    peers = [sibling, up, down]
    for off in range(1, 4):
        peers.append({"seq": at_g(lax.rem(g + off, NG))})
        peers.append({"seq": at_l(lax.rem(l + off, NL))})
        peers.append({"seq": at_x(lax.rem(x + off, NX))})
    n_seq = lax.axis_size("seq")
    after = {"seq": lax.rem(me + 1, n_seq)}
    before = {"seq": lax.rem(me + n_seq - 1, n_seq)}
    peers += [after, before]
    signal_all(peers)

    def remote(src, dst, send, recv, device):
        return pltpu.make_async_remote_copy(
            src_ref=src, dst_ref=dst, send_sem=send, recv_sem=recv,
            device_id=device, device_id_type=MESH,
        )

    T = k.shape[0]
    nc = T // C
    qc, kc, vc = q.shape[1], k.shape[1], v.shape[1]
    nk, nv = kc // C, vc // C
    rep = nv // nk
    sl = lambda c: slice(c * C, (c + 1) * C)

    loads[0].wait()
    loads[1].wait()
    row = lax.broadcasted_iota(jnp.int32, (T, T), 0)
    col = lax.broadcasted_iota(jnp.int32, (T, T), 1)
    upto = (row <= col).astype(BF)
    dec = -softplus(dl_v[...])
    d1 = dec.astype(BF)
    r = dec - d1.astype(F32)
    d2 = r.astype(BF)
    d3 = (r - d2.astype(F32)).astype(BF)
    lfr = bdot(d1, upto) + bdot(d2, upto) + bdot(d3, upto)
    last = lfr[:, T - 1 : T]
    cols_s[0:4, :] = 1.0 / (1.0 + jnp.exp(-bl_v[...]))
    cols_s[4:8, :] = lfr
    cols_s[8:12, :] = jnp.exp(lfr)
    cols_s[12:16, :] = jnp.exp(last - lfr)
    cols = jnp.transpose(cols_s[...])
    beta = lambda h, c: cols[sl(c), h : h + 1]
    lf = lambda h, c: cols[sl(c), 4 + h : 5 + h]
    ex = lambda h, c: cols[sl(c), 8 + h : 9 + h]
    tail = lambda h, c: cols[sl(c), 12 + h : 13 + h]
    f1 = jnp.exp(last) - 1.0

    ri = lax.broadcasted_iota(jnp.int32, (C, C), 0)
    ci = lax.broadcasted_iota(jnp.int32, (C, C), 1)
    eye = (ri == ci).astype(F32)
    strict = ri > ci
    within = ri >= ci

    wait_all(len(peers))
    sent_halo = []
    lo = 0
    for i, ref in enumerate((q, k, v)):
        span = pl.ds(lo, ref.shape[1])
        sent_halo.append(
            remote(ref.at[pl.ds(T - HALO, HALO)], halo_v.at[:, span], sh.at[i], rh.at[i], after)
        )
        lo += ref.shape[1]
    for copy in sent_halo:
        copy.start()
    sent_w = remote(w, w_sib, sw.at[0], rw.at[0], sibling)
    sent_w.start()

    def put(lo, raw):
        wide = raw.shape[1]
        ext[8 : 8 + T, lo : lo + wide] = raw[...].astype(F32)

    def conv(lo, taps, at, c, n=1):
        s = taps[0:1, at : at + C] * ext[5 + c * C : 5 + (c + n) * C, lo : lo + C]
        for j in range(1, 4):
            s = s + taps[j : j + 1, at : at + C] * ext[5 + j + c * C : 5 + j + (c + n) * C, lo : lo + C]
        return silu(s)

    for i in range(2, 6):
        loads[i].wait()
    put(qc, k_v)
    put(qc + kc, v_v)
    ks, kT, vs, KK, G, A = {}, {}, {}, {}, {}, {}

    def block(c):
        for j in range(nk):
            kj = conv(qc + j * C, kt_v, j * C, c)
            kj = kj * lax.rsqrt(jnp.sum(kj * kj, -1, keepdims=True) + EPS)
            ks[j, c] = kj.astype(BF)
            kT[j, c] = jnp.transpose(kj).astype(BF)
        for h in range(nv):
            vs[h, c] = conv(qc + kc + h * C, vt_v, h * C, c)

    def system(c, e):
        for j in range(nk):
            KK[j] = bdot_nt(ks[j, c], ks[j, e])
        for h in range(nv):
            G[h, c, e] = jnp.exp(jnp.minimum(lf(h, c) - lfr[h : h + 1, sl(e)], 0.0))
            a = (beta(h, c) * G[h, c, e]) * KK[h // rep]
            A[h, c, e] = jnp.where(strict, a, 0.0) if c == e else a

    def corner(s):
        return ((ri // (2 * s)) == (ci // (2 * s))) & ((ri // s) % 2 == 1) & ((ci // s) % 2 == 0)

    def inverses(keys):
        m = corner(1)
        out = {(h, c): eye - jnp.where(m, A[h, c, c], 0.0) for h, c in keys}
        s = 2
        while s < C:
            m = corner(s)
            part = {(h, c): bdot(jnp.where(m, A[h, c, c], 0.0), out[h, c]) for h, c in keys}
            out = {key: out[key] - bdot(out[key], part[key]) for key in keys}
            s *= 2
        return out

    for c in range(1, nc):
        block(c)
    for c in range(1, nc):
        for e in range(1, c + 1):
            system(c, e)
    inv = inverses([(h, c) for h in range(nv) for c in range(1, nc)])
    for copy in sent_halo:
        copy.wait_recv()
    start = halo_v[HALO - 3 : HALO, :].astype(F32)
    ext[5:8, :] = jnp.where(me > 0, start, jnp.zeros_like(start))
    block(0)
    for c in range(nc):
        system(c, 0)
    inv.update(inverses([(h, 0) for h in range(nv)]))

    X = {}
    for c in range(nc):
        rhs = {}
        for h in range(nv):
            kf = ks[h // rep, c].astype(F32)
            R = jnp.concatenate([beta(h, c) * vs[h, c], (beta(h, c) * ex(h, c)) * kf], 1)
            for e in range(c):
                R = R - bdot(A[h, c, e], X[h, e])
            rhs[h] = R
        for h in range(nv):
            X[h, c] = bdot(inv[h, c], rhs[h])
    for h in range(nv):
        hw = bdot(kT[h // rep, 0], tail(h, 0) * X[h, 0])
        for c in range(1, nc):
            hw = hw + bdot(kT[h // rep, c], tail(h, c) * X[h, c])
        pair[h, :, :C] = (f1[h : h + 1, :] * eye - hw[:, C:]).astype(BF)
        pair[h, :, C:] = hw[:, :C].astype(BF)

    c1, w1 = exchange(l, at_l, lambda i: pair.at[i], buf1, s1, r1)
    buf1[l] = pair[l]

    loads[6].wait()
    loads[7].wait()
    put(0, q_v)
    for j in range(nk):
        qj = conv(j * C, qt_v, j * C, 0, nc)
        qb = qj.astype(BF)
        for c in range(nc):
            QK = {e: bdot_nt(qb[sl(c)], ks[j, e]) for e in range(c + 1)}
            for h in range(j * rep, (j + 1) * rep):
                ow = None
                for e in range(c + 1):
                    sc = G[h, c, e] * QK[e]
                    if c == e:
                        sc = jnp.where(within, sc, 0.0)
                    p = bdot(sc, X[h, e])
                    ow = p if ow is None else ow + p
                oloc[h, sl(c), :] = ow[:, :C]
                qeff[h, sl(c), :] = (ex(h, c) * qj[sl(c)] - ow[:, C:]).astype(BF)

    for copy in w1:
        copy.wait_recv()
    e0, e1, e2, e3 = [buf1[i].astype(F32) for i in range(NL)]
    p2 = compose(e1, e0)
    tot[...] = compose(compose(e3, e2), p2).astype(BF)
    c2, w2 = exchange(g, at_g, lambda i: tot, buf2, s2, r2)
    buf2[g] = tot[...]
    p3 = compose(e2, p2)

    loads[8].wait()
    loads[9].wait()
    for h in range(nv):
        gs[:, sl(h)] = gain_v[...] * silu(gate_v[:, sl(h)].astype(F32))

    for copy in w2:
        copy.wait_recv()
    g0, g1, g2, g3 = [buf2[i].astype(F32) for i in range(NG)]
    q2 = compose(g1, g0)
    rowt[...] = compose(compose(g3, g2), q2).astype(BF)
    c3, w3 = exchange(x, at_x, lambda i: rowt, buf3, s3, r3)
    buf3[x] = rowt[...]
    q3 = compose(g2, q2)
    zero = jnp.zeros((C, 2 * C), F32)
    gp = jnp.where(g == 0, zero, jnp.where(g == 1, g0, jnp.where(g == 2, q2, q3)))
    full = [gp] + [compose(p, gp) for p in (e0, p2, p3)]

    for copy in w3:
        copy.wait_recv()
    state1 = buf3[0, :, C:].astype(F32)
    state2 = applied(buf3[1].astype(F32), state1)
    state3 = applied(buf3[2].astype(F32), state2)
    row_in = jnp.where(
        x == 0, zero[:, :C], jnp.where(x == 1, state1, jnp.where(x == 2, state2, state3))
    )
    for i in range(NL):
        outb[i] = applied(full[i], row_in).astype(BF)
    c4, w4 = exchange(l, at_l, lambda i: outb.at[i], sin, s4, r4)
    sin[l] = outb[l]
    loads[10].wait()
    for copy in w4:
        copy.wait_recv()

    rows = T // 8
    wide = w.shape[1] // CH
    half = nv * C // 2
    swap = [remote(nrm.at[i, 1 - core], n_sib.at[i], sa.at[i], ra.at[i], sibling) for i in range(2)]
    for i in range(2):
        for h in range(i * nv // 2, (i + 1) * nv // 2):
            o = oloc[h] + bdot(qeff[h], sin[h])
            o = o * lax.rsqrt(jnp.mean(o * o, -1, keepdims=True) + EPS)
            o = (o * gs[:, sl(h)]).astype(BF)
            at = h * C - i * half
            for b in range(8):
                nrm[i, b % 2, b // 2, :, at : at + C] = o[b * rows : (b + 1) * rows]
        swap[i].start()

    def lhs(ref):
        return ref.reshape(NY * rows, half)

    mine = jnp.concatenate([lhs(nrm[0, core]), lhs(nrm[1, core])], 1)
    for n in range(CH):
        acc[:, n * wide : (n + 1) * wide] = bdot(mine, w_v[:, n * wide : (n + 1) * wide])
    sent_w.wait_recv()
    for copy in swap:
        copy.wait_recv()
    other = jnp.concatenate([lhs(n_sib[0]), lhs(n_sib[1])], 1)

    y_up, y_down, y_far = lax.rem(y + 1, NY), lax.rem(y + NY - 1, NY), lax.rem(y + 2, NY)
    far, direct, last_hop = [], [], []
    for n in range(CH):
        a_dev, b_dev = (up, down) if n % 2 == 0 else (down, up)
        a_y, b_y = (y_up, y_down) if n % 2 == 0 else (y_down, y_up)
        a_land, b_land = (from_lo, from_hi) if n % 2 == 0 else (from_hi, from_lo)
        far.append(remote(psum.at[n, y_far], relay.at[n], sr.at[n], rr.at[n], a_dev))
        direct.append(remote(psum.at[n, b_y], b_land.at[n], sd.at[n], rd.at[n], b_dev))
        last_hop.append(remote(final_s.at[n], a_land.at[n], sf.at[n], rf.at[n], a_dev))
    for n in range(CH):
        at = slice(n * wide, (n + 1) * wide)
        total = acc[:, at] + bdot(other, w_sib[:, at])
        psum[n] = total.astype(BF).reshape(NY, rows, wide)
        far[n].start()
    for n in range(CH):
        direct[n].start()
    for n in range(CH):
        a_y = y_up if n % 2 == 0 else y_down
        far[n].wait_recv()
        final_s[n] = (psum[n, a_y].astype(F32) + relay[n].astype(F32)).astype(BF)
        last_hop[n].start()
    for n in range(CH):
        direct[n].wait_recv()
        last_hop[n].wait_recv()
        t = psum[n, y].astype(F32) + from_lo[n].astype(F32) + from_hi[n].astype(F32)
        out[:, n * wide : (n + 1) * wide] = t.astype(BF)
    for copy in sent_halo + [sent_w] + c1 + c2 + c3 + c4 + swap + far + direct + last_hop:
        copy.wait_send()


def shards(q, k, v, gate, qt, kt, vt, bl, dl, gain, w):
    D = pltpu.SemaphoreType.DMA
    V = pltpu.VMEM
    hbm = pl.BlockSpec(memory_space=pltpu.HBM)
    vmem = pl.BlockSpec(memory_space=pltpu.VMEM)
    T = q.shape[0]
    wide_in = q.shape[1] + k.shape[1] + v.shape[1]
    args = (q, k, v, gate, qt, kt, vt, bl.T, dl.T, gain.reshape(1, C), w)
    nv = v.shape[1] // C
    r, wide = T // 8, w.shape[1] // CH
    chunk = V((CH, r, wide), BF)
    four = V((CH, NY, r, wide), BF)
    scratch = [V(a.shape, a.dtype) for a in args]
    scratch += [D((len(args),)), V((HALO, wide_in), BF), V(w.shape, BF)]
    scratch += [D((3,)), D((3,)), D((1,)), D((1,))]
    scratch += [
        V((T + 8, wide_in), F32), V((16, T), F32), V((nv, T, C), F32), V((nv, T, C), BF),
        V((nv, C, 2 * C), BF), V((T, nv * C), F32),
    ]
    slots = V((4, C, 2 * C), BF)
    scratch += [slots, V((C, 2 * C), BF), slots, V((C, 2 * C), BF), slots]
    scratch += [V((4, C, C), BF), V((4, C, C), BF)]
    scratch += [D((3,)), D((4,))] * 4
    scratch += [V((2, 2, NY, r, nv * C // 2), BF), V((2, NY, r, nv * C // 2), BF)]
    scratch += [V((NY * r, w.shape[1]), F32), four]
    scratch += [chunk] * 4 + [D((2,))] * 2 + [D((CH,))] * 6
    return pl.pallas_call(
        layer_kernel,
        out_shape=jax.ShapeDtypeStruct((r, w.shape[1]), BF),
        in_specs=[hbm] * len(args),
        out_specs=vmem,
        scratch_shapes=scratch,
        compiler_params=pltpu.CompilerParams(
            collective_id=2, has_side_effects=True, vmem_limit_bytes=48 << 20
        ),
        name="layer",
    )(*[pltpu.with_memory_space_constraint(a, pltpu.HBM) for a in args])


def solution(mesh):
    tokens_heads = P("seq", "head")
    placed = (tokens_heads,) * 4 + (P(None, "head"),) * 3 + (tokens_heads,) * 2
    return jax.shard_map(
        shards,
        mesh=mesh,
        in_specs=placed + (P(), P("head", None)),
        out_specs=P(("seq", "head"), None),
        check_vma=False,
    )
```

```python
import jax
import jax.numpy as jnp
from jax import lax
from jax.experimental import pallas as pl
from jax.experimental.pallas import tpu as pltpu
from jax.sharding import PartitionSpec as P

EPS = 1e-6
F32 = jnp.float32
BF = jnp.bfloat16
MESH = pl.DeviceIdType.MESH
C = 128
NL = 4
NG = 4
NX = 4
NY = 4
CH = 4
HALO = 16
EDGE = 8


def bdot(a, b):
    return lax.dot_general(
        a.astype(BF), b.astype(BF), (((1,), (0,)), ((), ())), preferred_element_type=F32
    )


def bdot_nt(a, b):
    return lax.dot_general(
        a.astype(BF), b.astype(BF), (((1,), (1,)), ((), ())), preferred_element_type=F32
    )


def silu(x):
    return x / (1.0 + jnp.exp(-x))


def softplus(x):
    e = jnp.exp(-jnp.abs(x))
    u = 1.0 + e
    log1p = jnp.where(u == 1.0, e, jnp.log(u) * e / jnp.where(u == 1.0, 1.0, u - 1.0))
    return jnp.maximum(x, 0.0) + log1p


def compose(later, earlier):
    return later + earlier + bdot(later[:, :C], earlier)


def applied(pair, state):
    return state + pair[:, C:] + bdot(pair[:, :C], state)


def place():
    me = lax.axis_index("seq")
    return me, lax.rem(me, NL), lax.rem(me // NL, NG), me // (NL * NG)


def signal_all(devices):
    barrier = pltpu.get_barrier_semaphore()
    for d in devices:
        pl.semaphore_signal(barrier, inc=1, device_id=d, device_id_type=MESH)


def wait_all(count):
    pl.semaphore_wait(pltpu.get_barrier_semaphore(), count)


def exchange(slot, device_of, src_of, land, send, recv):
    def copy(off, at):
        to = lax.rem(slot + off, 4)
        return pltpu.make_async_remote_copy(
            src_ref=src_of(to),
            dst_ref=land.at[at(to)],
            send_sem=send.at[off - 1],
            recv_sem=recv.at[at(to)],
            device_id={"seq": device_of(to)},
            device_id_type=MESH,
        )

    out = [copy(off, lambda to: slot) for off in range(1, 4)]
    for c in out:
        c.start()
    return out, [copy(off, lambda to: to) for off in range(1, 4)]


def layer_kernel(
    q, k, v, gate, qt, kt, vt, blt, dlt, gain, w,
    out,
    q_v, k_v, v_v, gate_v, qt_v, kt_v, vt_v, bl_v, dl_v, gain_v, w_v, in_sem,
    halo_v, w_sib, sh, rh, sw, rw,
    ext, cols_s, oloc, qeff, pair, gs,
    buf1, tot, buf2, rowt, buf3, outb, sin,
    s1, r1, s2, r2, s3, r3, s4, r4,
    nrm, n_sib, psum, relay, final_s, from_lo, from_hi,
    sa, ra, sr, rr, sd, rd, sf, rf,
):
    pairs_in = (
        (dlt, dl_v), (blt, bl_v), (kt, kt_v), (k, k_v), (vt, vt_v), (v, v_v),
        (qt, qt_v), (q, q_v), (gate, gate_v), (gain, gain_v), (w, w_v),
    )
    loads = {}
    for i, (src, dst) in enumerate(pairs_in):
        loads[i] = pltpu.make_async_copy(src, dst, in_sem.at[i])
        loads[i].start()
    me, l, g, x = place()
    hd = lax.axis_index("head")
    y, core = hd // 2, lax.rem(hd, 2)
    at_l = lambda i: me - l + i
    at_g = lambda i: me + (i - g) * NL
    at_x = lambda i: me + (i - x) * (NL * NG)
    sibling = {"head": hd + 1 - 2 * core}
    up = {"head": 2 * lax.rem(y + 1, NY) + core}
    down = {"head": 2 * lax.rem(y + NY - 1, NY) + core}
    peers = [sibling, up, down]
    for off in range(1, 4):
        peers.append({"seq": at_g(lax.rem(g + off, NG))})
        peers.append({"seq": at_l(lax.rem(l + off, NL))})
        peers.append({"seq": at_x(lax.rem(x + off, NX))})
    n_seq = lax.axis_size("seq")
    after = {"seq": lax.rem(me + 1, n_seq)}
    before = {"seq": lax.rem(me + n_seq - 1, n_seq)}
    peers += [after, before]
    signal_all(peers)

    def remote(src, dst, send, recv, device):
        return pltpu.make_async_remote_copy(
            src_ref=src, dst_ref=dst, send_sem=send, recv_sem=recv,
            device_id=device, device_id_type=MESH,
        )

    T = k.shape[0]
    nc = T // C
    qc, kc, vc = q.shape[1], k.shape[1], v.shape[1]
    nk, nv = kc // C, vc // C
    rep = nv // nk
    sl = lambda c: slice(c * C, (c + 1) * C)

    loads[0].wait()
    loads[1].wait()
    row = lax.broadcasted_iota(jnp.int32, (T, T), 0)
    col = lax.broadcasted_iota(jnp.int32, (T, T), 1)
    upto = (row <= col).astype(BF)
    dec = -softplus(dl_v[...])
    d1 = dec.astype(BF)
    r = dec - d1.astype(F32)
    d2 = r.astype(BF)
    d3 = (r - d2.astype(F32)).astype(BF)
    lfr = bdot(d1, upto) + bdot(d2, upto) + bdot(d3, upto)
    last = lfr[:, T - 1 : T]
    cols_s[0:4, :] = 1.0 / (1.0 + jnp.exp(-bl_v[...]))
    cols_s[4:8, :] = lfr
    cols_s[8:12, :] = jnp.exp(lfr)
    cols_s[12:16, :] = jnp.exp(last - lfr)
    cols = jnp.transpose(cols_s[...])
    beta = lambda h, c: cols[sl(c), h : h + 1]
    lf = lambda h, c: cols[sl(c), 4 + h : 5 + h]
    ex = lambda h, c: cols[sl(c), 8 + h : 9 + h]
    tail = lambda h, c: cols[sl(c), 12 + h : 13 + h]
    f1 = jnp.exp(last) - 1.0

    ri = lax.broadcasted_iota(jnp.int32, (C, C), 0)
    ci = lax.broadcasted_iota(jnp.int32, (C, C), 1)
    eye = (ri == ci).astype(F32)
    strict = ri > ci
    within = ri >= ci

    wait_all(len(peers))
    sent_halo = []
    lo = 0
    for i, ref in enumerate((q, k, v)):
        span = pl.ds(lo, ref.shape[1])
        sent_halo.append(
            remote(ref.at[pl.ds(T - HALO, HALO)], halo_v.at[:, span], sh.at[i], rh.at[i], after)
        )
        lo += ref.shape[1]
    for copy in sent_halo:
        copy.start()
    sent_w = remote(w, w_sib, sw.at[0], rw.at[0], sibling)
    sent_w.start()

    def put(lo, raw):
        wide = raw.shape[1]
        ext[8 : 8 + T, lo : lo + wide] = raw[...].astype(F32)

    def conv(lo, taps, at, c, n=1):
        s = taps[0:1, at : at + C] * ext[5 + c * C : 5 + (c + n) * C, lo : lo + C]
        for j in range(1, 4):
            s = s + taps[j : j + 1, at : at + C] * ext[5 + j + c * C : 5 + j + (c + n) * C, lo : lo + C]
        return silu(s)

    for i in range(2, 6):
        loads[i].wait()
    put(qc, k_v)
    put(qc + kc, v_v)
    ks, kT, vs, KK, G, A = {}, {}, {}, {}, {}, {}

    def block(c):
        for j in range(nk):
            kj = conv(qc + j * C, kt_v, j * C, c)
            kj = kj * lax.rsqrt(jnp.sum(kj * kj, -1, keepdims=True) + EPS)
            ks[j, c] = kj.astype(BF)
            kT[j, c] = jnp.transpose(kj).astype(BF)
        for h in range(nv):
            vs[h, c] = conv(qc + kc + h * C, vt_v, h * C, c)

    def system(c, e):
        for j in range(nk):
            KK[j] = bdot_nt(ks[j, c], ks[j, e])
        for h in range(nv):
            G[h, c, e] = jnp.exp(jnp.minimum(lf(h, c) - lfr[h : h + 1, sl(e)], 0.0))
            a = (beta(h, c) * G[h, c, e]) * KK[h // rep]
            A[h, c, e] = jnp.where(strict, a, 0.0) if c == e else a

    def corner(s):
        return ((ri // (2 * s)) == (ci // (2 * s))) & ((ri // s) % 2 == 1) & ((ci // s) % 2 == 0)

    def inverses(blocks, upto=C):
        m = corner(1)
        out = {key: eye - jnp.where(m, a, 0.0) for key, a in blocks.items()}
        s = 2
        while s < upto:
            m = corner(s)
            part = {key: bdot(jnp.where(m, a, 0.0), out[key]) for key, a in blocks.items()}
            out = {key: out[key] - bdot(out[key], part[key]) for key in blocks}
            s *= 2
        return out

    def rhs(h, c):
        kf = ks[h // rep, c].astype(F32)
        return jnp.concatenate([beta(h, c) * vs[h, c], (beta(h, c) * ex(h, c)) * kf], 1)

    ext[0:8, :] = jnp.zeros((8, ext.shape[1]), F32)
    inner = (ri >= EDGE) & (ci >= EDGE)
    for c in range(nc):
        block(c)
    for c in range(nc):
        for e in range(min(c, 1), c + 1):
            system(c, e)
    blocks = {(h, c): A[h, c, c] for h in range(nv) for c in range(1, nc)}
    blocks.update({(h, 0): jnp.where(inner, A[h, 0, 0], 0.0) for h in range(nv)})
    inv = inverses(blocks)
    ahead, cross = {}, {}
    for h in range(nv):
        cross[h] = bdot(inv[h, 2], bdot(A[h, 2, 1], inv[h, 1]))
    for h in range(nv):
        b1, b2 = rhs(h, 1), rhs(h, 2)
        ahead[h, 1] = bdot(inv[h, 1], b1)
        ahead[h, 2] = bdot(inv[h, 2], b2) - bdot(cross[h], b1)

    for copy in sent_halo:
        copy.wait_recv()
    start = halo_v[HALO - 3 : HALO, :].astype(F32)
    ext[5:8, :] = jnp.where(me > 0, start, jnp.zeros_like(start))
    block(0)
    for c in range(nc):
        system(c, 0)
    edge = inverses({h: jnp.where(ri < EDGE, A[h, 0, 0], 0.0) for h in range(nv)}, EDGE)
    X = {}
    part = {h: bdot(edge[h], rhs(h, 0)) for h in range(nv)}
    for h in range(nv):
        below = jnp.where((ri >= EDGE) & (ci < EDGE), A[h, 0, 0], 0.0)
        part[h] = part[h] - bdot(below, part[h])
    for h in range(nv):
        X[h, 0] = bdot(inv[h, 0], part[h])
    for h in range(nv):
        b1, b2 = bdot(A[h, 1, 0], X[h, 0]), bdot(A[h, 2, 0], X[h, 0])
        X[h, 1] = ahead[h, 1] - bdot(inv[h, 1], b1)
        X[h, 2] = ahead[h, 2] - bdot(inv[h, 2], b2) + bdot(cross[h], b1)
    for h in range(nv):
        hw = bdot(kT[h // rep, 0], tail(h, 0) * X[h, 0])
        for c in range(1, nc):
            hw = hw + bdot(kT[h // rep, c], tail(h, c) * X[h, c])
        pair[h, :, :C] = (f1[h : h + 1, :] * eye - hw[:, C:]).astype(BF)
        pair[h, :, C:] = hw[:, :C].astype(BF)

    c1, w1 = exchange(l, at_l, lambda i: pair.at[i], buf1, s1, r1)
    buf1[l] = pair[l]

    loads[6].wait()
    loads[7].wait()
    put(0, q_v)
    for j in range(nk):
        qj = conv(j * C, qt_v, j * C, 0, nc)
        qb = qj.astype(BF)
        for c in range(nc):
            QK = {e: bdot_nt(qb[sl(c)], ks[j, e]) for e in range(c + 1)}
            for h in range(j * rep, (j + 1) * rep):
                ow = None
                for e in range(c + 1):
                    sc = G[h, c, e] * QK[e]
                    if c == e:
                        sc = jnp.where(within, sc, 0.0)
                    p = bdot(sc, X[h, e])
                    ow = p if ow is None else ow + p
                oloc[h, sl(c), :] = ow[:, :C]
                qeff[h, sl(c), :] = (ex(h, c) * qj[sl(c)] - ow[:, C:]).astype(BF)

    for copy in w1:
        copy.wait_recv()
    e0, e1, e2, e3 = [buf1[i].astype(F32) for i in range(NL)]
    p2 = compose(e1, e0)
    tot[...] = compose(compose(e3, e2), p2).astype(BF)
    c2, w2 = exchange(g, at_g, lambda i: tot, buf2, s2, r2)
    buf2[g] = tot[...]
    p3 = compose(e2, p2)

    loads[8].wait()
    loads[9].wait()
    for h in range(nv):
        gs[:, sl(h)] = gain_v[...] * silu(gate_v[:, sl(h)].astype(F32))

    for copy in w2:
        copy.wait_recv()
    g0, g1, g2, g3 = [buf2[i].astype(F32) for i in range(NG)]
    q2 = compose(g1, g0)
    rowt[...] = compose(compose(g3, g2), q2).astype(BF)
    c3, w3 = exchange(x, at_x, lambda i: rowt, buf3, s3, r3)
    buf3[x] = rowt[...]
    q3 = compose(g2, q2)
    zero = jnp.zeros((C, 2 * C), F32)
    gp = jnp.where(g == 0, zero, jnp.where(g == 1, g0, jnp.where(g == 2, q2, q3)))
    full = [gp] + [compose(p, gp) for p in (e0, p2, p3)]

    for copy in w3:
        copy.wait_recv()
    after0 = buf3[0, :, C:].astype(F32)
    after1 = applied(buf3[1].astype(F32), after0)
    early = jnp.where(x == 2, after0, jnp.where(x == 3, after1, jnp.zeros_like(after0)))
    late = buf3[lax.rem(x + NX - 1, NX)].astype(F32)
    late = jnp.where(x > 0, late, jnp.zeros_like(late))
    through = [compose(p, late) for p in full]
    for i in range(NL):
        outb[i] = applied(through[i], early).astype(BF)
    c4, w4 = exchange(l, at_l, lambda i: outb.at[i], sin, s4, r4)
    sin[l] = outb[l]
    loads[10].wait()
    for copy in w4:
        copy.wait_recv()

    rows = T // 8
    wide = w.shape[1] // CH
    y_up, y_down, y_far = lax.rem(y + 1, NY), lax.rem(y + NY - 1, NY), lax.rem(y + 2, NY)

    swap = [
        remote(nrm.at[1 - core, pl.ds(0, 1)], n_sib.at[pl.ds(0, 1)], sa.at[0], ra.at[0], sibling),
        remote(nrm.at[1 - core, pl.ds(1, 3)], n_sib.at[pl.ds(1, 3)], sa.at[1], ra.at[1], sibling),
    ]

    def normed(at, slot):
        span = pl.ds(pl.multiple_of(at * 2 * rows, 2 * rows), 2 * rows)
        for h in range(nv):
            o = oloc[h, span, :] + bdot(qeff[h, span, :], sin[h])
            o = o * lax.rsqrt(jnp.mean(o * o, -1, keepdims=True) + EPS)
            o = (o * gs[span, sl(h)]).astype(BF)
            for b in range(2):
                nrm[b, slot, :, sl(h)] = o[b * rows : (b + 1) * rows]

    def project(lo, hi, n):
        at = slice(n * wide, (n + 1) * wide)
        count = (hi - lo) * rows
        mine = nrm[core, lo:hi].reshape(count, nv * C)
        other = n_sib[lo:hi].reshape(count, nv * C)
        total = bdot(mine, w_v[:, at]) + bdot(other, w_sib[:, at])
        psum[n, lo:hi] = total.astype(BF).reshape(hi - lo, rows, wide)

    far, direct, last_hop = [], [], []
    for n in range(CH):
        a_dev, b_dev = (up, down) if n % 2 == 0 else (down, up)
        b_slot = 2 if n % 2 == 0 else 1
        a_land, b_land = (from_lo, from_hi) if n % 2 == 0 else (from_hi, from_lo)
        far.append(remote(psum.at[n, 0], relay.at[n], sr.at[n], rr.at[n], a_dev))
        direct.append(remote(psum.at[n, b_slot], b_land.at[n], sd.at[n], rd.at[n], b_dev))
        last_hop.append(remote(final_s.at[n], a_land.at[n], sf.at[n], rf.at[n], a_dev))
    normed(y_far, 0)
    swap[0].start()
    for slot, at in ((1, y_up), (2, y_down), (3, y)):
        normed(at, slot)
    swap[1].start()
    sent_w.wait_recv()
    swap[0].wait_recv()
    for n in range(CH):
        project(0, 1, n)
        far[n].start()
    swap[1].wait_recv()
    for n in range(CH):
        project(1, NY, n)
        direct[n].start()
    for n in range(CH):
        a_slot = 1 if n % 2 == 0 else 2
        far[n].wait_recv()
        final_s[n] = (psum[n, a_slot].astype(F32) + relay[n].astype(F32)).astype(BF)
        last_hop[n].start()
    for n in range(CH):
        direct[n].wait_recv()
        last_hop[n].wait_recv()
        t = psum[n, 3].astype(F32) + from_lo[n].astype(F32) + from_hi[n].astype(F32)
        out[:, n * wide : (n + 1) * wide] = t.astype(BF)
    for copy in sent_halo + [sent_w] + c1 + c2 + c3 + c4 + swap + far + direct + last_hop:
        copy.wait_send()


def shards(q, k, v, gate, qt, kt, vt, bl, dl, gain, w):
    D = pltpu.SemaphoreType.DMA
    V = pltpu.VMEM
    hbm = pl.BlockSpec(memory_space=pltpu.HBM)
    vmem = pl.BlockSpec(memory_space=pltpu.VMEM)
    T = q.shape[0]
    wide_in = q.shape[1] + k.shape[1] + v.shape[1]
    args = (q, k, v, gate, qt, kt, vt, bl.T, dl.T, gain.reshape(1, C), w)
    nv = v.shape[1] // C
    r, wide = T // 8, w.shape[1] // CH
    chunk = V((CH, r, wide), BF)
    four = V((CH, NY, r, wide), BF)
    scratch = [V(a.shape, a.dtype) for a in args]
    scratch += [D((len(args),)), V((HALO, wide_in), BF), V(w.shape, BF)]
    scratch += [D((3,)), D((3,)), D((1,)), D((1,))]
    scratch += [
        V((T + 8, wide_in), F32), V((16, T), F32), V((nv, T, C), F32), V((nv, T, C), BF),
        V((nv, C, 2 * C), BF), V((T, nv * C), F32),
    ]
    slots = V((4, C, 2 * C), BF)
    scratch += [slots, V((C, 2 * C), BF), slots, V((C, 2 * C), BF), slots]
    scratch += [V((4, C, C), BF), V((4, C, C), BF)]
    scratch += [D((3,)), D((4,))] * 4
    scratch += [V((2, NY, r, nv * C), BF), V((NY, r, nv * C), BF), four]
    scratch += [chunk] * 4 + [D((2,))] * 2 + [D((CH,))] * 6
    return pl.pallas_call(
        layer_kernel,
        out_shape=jax.ShapeDtypeStruct((r, w.shape[1]), BF),
        in_specs=[hbm] * len(args),
        out_specs=vmem,
        scratch_shapes=scratch,
        compiler_params=pltpu.CompilerParams(
            collective_id=2, has_side_effects=True, vmem_limit_bytes=48 << 20
        ),
        name="layer",
    )(*[pltpu.with_memory_space_constraint(a, pltpu.HBM) for a in args])


def solution(mesh):
    tokens_heads = P("seq", "head")
    placed = (tokens_heads,) * 4 + (P(None, "head"),) * 3 + (tokens_heads,) * 2
    return jax.shard_map(
        shards,
        mesh=mesh,
        in_specs=placed + (P(), P("head", None)),
        out_specs=P(("seq", "head"), None),
        check_vma=False,
    )
```

```python
import jax
import jax.numpy as jnp
from jax import lax
from jax.experimental import pallas as pl
from jax.experimental.pallas import tpu as pltpu
from jax.sharding import PartitionSpec as P

EPS = 1e-6
F32 = jnp.float32
BF = jnp.bfloat16
MESH = pl.DeviceIdType.MESH
C = 128
NL = 4
NG = 4
NX = 4
NY = 4
CH = 4
HALO = 16
EDGE = 8


def bdot(a, b):
    return lax.dot_general(
        a.astype(BF), b.astype(BF), (((1,), (0,)), ((), ())), preferred_element_type=F32
    )


def bdot_nt(a, b):
    return lax.dot_general(
        a.astype(BF), b.astype(BF), (((1,), (1,)), ((), ())), preferred_element_type=F32
    )


def silu(x):
    return x / (1.0 + jnp.exp(-x))


def softplus(x):
    e = jnp.exp(-jnp.abs(x))
    u = 1.0 + e
    log1p = jnp.where(u == 1.0, e, jnp.log(u) * e / jnp.where(u == 1.0, 1.0, u - 1.0))
    return jnp.maximum(x, 0.0) + log1p


def compose(later, earlier):
    return later + earlier + bdot(later[:, :C], earlier)


def applied(pair, state):
    return state + pair[:, C:] + bdot(pair[:, :C], state)


def place():
    me = lax.axis_index("seq")
    return me, lax.rem(me, NL), lax.rem(me // NL, NG), me // (NL * NG)


def signal_all(devices):
    barrier = pltpu.get_barrier_semaphore()
    for d in devices:
        pl.semaphore_signal(barrier, inc=1, device_id=d, device_id_type=MESH)


def wait_all(count):
    pl.semaphore_wait(pltpu.get_barrier_semaphore(), count)


def exchange(slot, device_of, src_of, land, send, recv):
    def copy(off, at):
        to = lax.rem(slot + off, 4)
        return pltpu.make_async_remote_copy(
            src_ref=src_of(to),
            dst_ref=land.at[at(to)],
            send_sem=send.at[off - 1],
            recv_sem=recv.at[at(to)],
            device_id={"seq": device_of(to)},
            device_id_type=MESH,
        )

    out = [copy(off, lambda to: slot) for off in (2, 1, 3)]
    for c in out:
        c.start()
    return out, [copy(off, lambda to: to) for off in range(1, 4)]


def layer_kernel(
    q, k, v, gate, qt, kt, vt, blt, dlt, gain, w,
    out,
    q_v, k_v, v_v, gate_v, qt_v, kt_v, vt_v, bl_v, dl_v, gain_v, w_v, in_sem,
    halo_v, w_sib, sh, rh, sw, rw,
    ext, cols_s, oloc, qeff, pair, gs,
    buf1, tot, buf2, rowt, buf3, outb, sin,
    s1, r1, s2, r2, s3, r3, s4, r4,
    nrm, n_sib, psum, relay, final_s, from_lo, from_hi,
    sa, ra, sr, rr, sd, rd, sf, rf,
):
    pairs_in = (
        (dlt, dl_v), (blt, bl_v), (kt, kt_v), (k, k_v), (vt, vt_v), (v, v_v),
        (qt, qt_v), (q, q_v), (gate, gate_v), (gain, gain_v), (w, w_v),
    )
    loads = {}
    for i, (src, dst) in enumerate(pairs_in):
        loads[i] = pltpu.make_async_copy(src, dst, in_sem.at[i])
    for i in range(6):
        loads[i].start()
    me, l, g, x = place()
    hd = lax.axis_index("head")
    y, core = hd // 2, lax.rem(hd, 2)
    at_l = lambda i: me - l + i
    at_g = lambda i: me + (i - g) * NL
    at_x = lambda i: me + (i - x) * (NL * NG)
    sibling = {"head": hd + 1 - 2 * core}
    up = {"head": 2 * lax.rem(y + 1, NY) + core}
    down = {"head": 2 * lax.rem(y + NY - 1, NY) + core}
    peers = [sibling, up, down]
    for off in range(1, 4):
        peers.append({"seq": at_g(lax.rem(g + off, NG))})
        peers.append({"seq": at_l(lax.rem(l + off, NL))})
        peers.append({"seq": at_x(lax.rem(x + off, NX))})
    n_seq = lax.axis_size("seq")
    after = {"seq": lax.rem(me + 1, n_seq)}
    before = {"seq": lax.rem(me + n_seq - 1, n_seq)}
    peers += [after, before]
    signal_all(peers)

    def remote(src, dst, send, recv, device):
        return pltpu.make_async_remote_copy(
            src_ref=src, dst_ref=dst, send_sem=send, recv_sem=recv,
            device_id=device, device_id_type=MESH,
        )

    T = k.shape[0]
    nc = T // C
    qc, kc, vc = q.shape[1], k.shape[1], v.shape[1]
    nk, nv = kc // C, vc // C
    rep = nv // nk
    sl = lambda c: slice(c * C, (c + 1) * C)

    loads[0].wait()
    loads[1].wait()
    row = lax.broadcasted_iota(jnp.int32, (T, T), 0)
    col = lax.broadcasted_iota(jnp.int32, (T, T), 1)
    upto = (row <= col).astype(BF)
    dec = -softplus(dl_v[...])
    d1 = dec.astype(BF)
    r = dec - d1.astype(F32)
    d2 = r.astype(BF)
    d3 = (r - d2.astype(F32)).astype(BF)
    lfr = bdot(d1, upto) + bdot(d2, upto) + bdot(d3, upto)
    last = lfr[:, T - 1 : T]
    cols_s[0:4, :] = 1.0 / (1.0 + jnp.exp(-bl_v[...]))
    cols_s[4:8, :] = lfr
    cols_s[8:12, :] = jnp.exp(lfr)
    cols_s[12:16, :] = jnp.exp(last - lfr)
    cols = jnp.transpose(cols_s[...])
    beta = lambda h, c: cols[sl(c), h : h + 1]
    lf = lambda h, c: cols[sl(c), 4 + h : 5 + h]
    ex = lambda h, c: cols[sl(c), 8 + h : 9 + h]
    tail = lambda h, c: cols[sl(c), 12 + h : 13 + h]
    f1 = jnp.exp(last) - 1.0

    ri = lax.broadcasted_iota(jnp.int32, (C, C), 0)
    ci = lax.broadcasted_iota(jnp.int32, (C, C), 1)
    eye = (ri == ci).astype(F32)
    strict = ri > ci
    within = ri >= ci

    wait_all(len(peers))
    sent_halo = []
    lo = 0
    for i, ref in enumerate((q, k, v)):
        span = pl.ds(lo, ref.shape[1])
        sent_halo.append(
            remote(ref.at[pl.ds(T - HALO, HALO)], halo_v.at[:, span], sh.at[i], rh.at[i], after)
        )
        lo += ref.shape[1]
    for copy in sent_halo:
        copy.start()
    for i in range(6, 11):
        loads[i].start()

    def put(lo, raw):
        wide = raw.shape[1]
        ext[8 : 8 + T, lo : lo + wide] = raw[...].astype(F32)

    def conv(lo, taps, at, c, n=1):
        s = taps[0:1, at : at + C] * ext[5 + c * C : 5 + (c + n) * C, lo : lo + C]
        for j in range(1, 4):
            s = s + taps[j : j + 1, at : at + C] * ext[5 + j + c * C : 5 + j + (c + n) * C, lo : lo + C]
        return silu(s)

    for i in range(2, 6):
        loads[i].wait()
    put(qc, k_v)
    put(qc + kc, v_v)
    ks, kT, vs, KK, G, A = {}, {}, {}, {}, {}, {}

    def block(c):
        for j in range(nk):
            kj = conv(qc + j * C, kt_v, j * C, c)
            kj = kj * lax.rsqrt(jnp.sum(kj * kj, -1, keepdims=True) + EPS)
            ks[j, c] = kj.astype(BF)
            kT[j, c] = jnp.transpose(kj).astype(BF)
        for h in range(nv):
            vs[h, c] = conv(qc + kc + h * C, vt_v, h * C, c)

    def system(c, e):
        for j in range(nk):
            KK[j] = bdot_nt(ks[j, c], ks[j, e])
        for h in range(nv):
            G[h, c, e] = jnp.exp(jnp.minimum(lf(h, c) - lfr[h : h + 1, sl(e)], 0.0))
            a = (beta(h, c) * G[h, c, e]) * KK[h // rep]
            A[h, c, e] = jnp.where(strict, a, 0.0) if c == e else a

    def corner(s):
        return ((ri // (2 * s)) == (ci // (2 * s))) & ((ri // s) % 2 == 1) & ((ci // s) % 2 == 0)

    def inverses(blocks, upto=C):
        m = corner(1)
        out = {key: eye - jnp.where(m, a, 0.0) for key, a in blocks.items()}
        s = 2
        while s < upto:
            m = corner(s)
            part = {key: bdot(jnp.where(m, a, 0.0), out[key]) for key, a in blocks.items()}
            out = {key: out[key] - bdot(out[key], part[key]) for key in blocks}
            s *= 2
        return out

    def rhs(h, c):
        kf = ks[h // rep, c].astype(F32)
        return jnp.concatenate([beta(h, c) * vs[h, c], (beta(h, c) * ex(h, c)) * kf], 1)

    ext[0:8, :] = jnp.zeros((8, ext.shape[1]), F32)
    inner = (ri >= EDGE) & (ci >= EDGE)
    for c in range(nc):
        block(c)
    for c in range(nc):
        for e in range(min(c, 1), c + 1):
            system(c, e)
    blocks = {(h, c): A[h, c, c] for h in range(nv) for c in range(1, nc)}
    blocks.update({(h, 0): jnp.where(inner, A[h, 0, 0], 0.0) for h in range(nv)})
    inv = inverses(blocks)
    ahead, cross = {}, {}
    for h in range(nv):
        cross[h] = bdot(inv[h, 2], bdot(A[h, 2, 1], inv[h, 1]))
    for h in range(nv):
        b1, b2 = rhs(h, 1), rhs(h, 2)
        ahead[h, 1] = bdot(inv[h, 1], b1)
        ahead[h, 2] = bdot(inv[h, 2], b2) - bdot(cross[h], b1)

    for copy in sent_halo:
        copy.wait_recv()
    start = halo_v[HALO - 3 : HALO, :].astype(F32)
    ext[5:8, :] = jnp.where(me > 0, start, jnp.zeros_like(start))
    block(0)
    for c in range(nc):
        system(c, 0)
    edge = inverses({h: jnp.where(ri < EDGE, A[h, 0, 0], 0.0) for h in range(nv)}, EDGE)
    X = {}
    part = {h: bdot(edge[h], rhs(h, 0)) for h in range(nv)}
    for h in range(nv):
        below = jnp.where((ri >= EDGE) & (ci < EDGE), A[h, 0, 0], 0.0)
        part[h] = part[h] - bdot(below, part[h])
    for h in range(nv):
        X[h, 0] = bdot(inv[h, 0], part[h])
    for h in range(nv):
        b1, b2 = bdot(A[h, 1, 0], X[h, 0]), bdot(A[h, 2, 0], X[h, 0])
        X[h, 1] = ahead[h, 1] - bdot(inv[h, 1], b1)
        X[h, 2] = ahead[h, 2] - bdot(inv[h, 2], b2) + bdot(cross[h], b1)
    for h in range(nv):
        hw = bdot(kT[h // rep, 0], tail(h, 0) * X[h, 0])
        for c in range(1, nc):
            hw = hw + bdot(kT[h // rep, c], tail(h, c) * X[h, c])
        pair[h, :, :C] = (f1[h : h + 1, :] * eye - hw[:, C:]).astype(BF)
        pair[h, :, C:] = hw[:, :C].astype(BF)

    c1, w1 = exchange(l, at_l, lambda i: pair.at[i], buf1, s1, r1)
    buf1[l] = pair[l]
    sent_w = remote(w, w_sib, sw.at[0], rw.at[0], sibling)
    sent_w.start()

    loads[6].wait()
    loads[7].wait()
    put(0, q_v)
    for j in range(nk):
        qj = conv(j * C, qt_v, j * C, 0, nc)
        qb = qj.astype(BF)
        for c in range(nc):
            QK = {e: bdot_nt(qb[sl(c)], ks[j, e]) for e in range(c + 1)}
            for h in range(j * rep, (j + 1) * rep):
                ow = None
                for e in range(c + 1):
                    sc = G[h, c, e] * QK[e]
                    if c == e:
                        sc = jnp.where(within, sc, 0.0)
                    p = bdot(sc, X[h, e])
                    ow = p if ow is None else ow + p
                oloc[h, sl(c), :] = ow[:, :C]
                qeff[h, sl(c), :] = (ex(h, c) * qj[sl(c)] - ow[:, C:]).astype(BF)

    for copy in w1:
        copy.wait_recv()
    e0, e1, e2, e3 = [buf1[i].astype(F32) for i in range(NL)]
    p2 = compose(e1, e0)
    tot[...] = compose(compose(e3, e2), p2).astype(BF)
    c2, w2 = exchange(g, at_g, lambda i: tot, buf2, s2, r2)
    buf2[g] = tot[...]
    p3 = compose(e2, p2)

    loads[8].wait()
    loads[9].wait()
    for h in range(nv):
        gs[:, sl(h)] = gain_v[...] * silu(gate_v[:, sl(h)].astype(F32))

    for copy in w2:
        copy.wait_recv()
    g0, g1, g2, g3 = [buf2[i].astype(F32) for i in range(NG)]
    q2 = compose(g1, g0)
    rowt[...] = compose(compose(g3, g2), q2).astype(BF)
    c3, w3 = exchange(x, at_x, lambda i: rowt, buf3, s3, r3)
    buf3[x] = rowt[...]
    q3 = compose(g2, q2)
    zero = jnp.zeros((C, 2 * C), F32)
    gp = jnp.where(g == 0, zero, jnp.where(g == 1, g0, jnp.where(g == 2, q2, q3)))
    full = [gp] + [compose(p, gp) for p in (e0, p2, p3)]

    for copy in w3:
        copy.wait_recv()
    after0 = buf3[0, :, C:].astype(F32)
    after1 = applied(buf3[1].astype(F32), after0)
    early = jnp.where(x == 2, after0, jnp.where(x == 3, after1, jnp.zeros_like(after0)))
    late = buf3[lax.rem(x + NX - 1, NX)].astype(F32)
    late = jnp.where(x > 0, late, jnp.zeros_like(late))
    through = [compose(p, late) for p in full]
    for i in range(NL):
        outb[i] = applied(through[i], early).astype(BF)
    c4, w4 = exchange(l, at_l, lambda i: outb.at[i], sin, s4, r4)
    sin[l] = outb[l]
    loads[10].wait()
    for copy in w4:
        copy.wait_recv()

    rows = T // 8
    wide = w.shape[1] // CH
    y_up, y_down, y_far = lax.rem(y + 1, NY), lax.rem(y + NY - 1, NY), lax.rem(y + 2, NY)

    swap = [
        remote(nrm.at[1 - core, pl.ds(0, 1)], n_sib.at[pl.ds(0, 1)], sa.at[0], ra.at[0], sibling),
        remote(nrm.at[1 - core, pl.ds(1, 3)], n_sib.at[pl.ds(1, 3)], sa.at[1], ra.at[1], sibling),
    ]

    def normed(at, slot):
        span = pl.ds(pl.multiple_of(at * 2 * rows, 2 * rows), 2 * rows)
        for h in range(nv):
            o = oloc[h, span, :] + bdot(qeff[h, span, :], sin[h])
            o = o * lax.rsqrt(jnp.mean(o * o, -1, keepdims=True) + EPS)
            o = (o * gs[span, sl(h)]).astype(BF)
            for b in range(2):
                nrm[b, slot, :, sl(h)] = o[b * rows : (b + 1) * rows]

    def project(lo, hi, n):
        at = slice(n * wide, (n + 1) * wide)
        count = (hi - lo) * rows
        mine = nrm[core, lo:hi].reshape(count, nv * C)
        other = n_sib[lo:hi].reshape(count, nv * C)
        total = bdot(mine, w_v[:, at]) + bdot(other, w_sib[:, at])
        psum[n, lo:hi] = total.astype(BF).reshape(hi - lo, rows, wide)

    far, direct, last_hop = [], [], []
    for n in range(CH):
        a_dev, b_dev = (up, down) if n % 2 == 0 else (down, up)
        b_slot = 2 if n % 2 == 0 else 1
        a_land, b_land = (from_lo, from_hi) if n % 2 == 0 else (from_hi, from_lo)
        far.append(remote(psum.at[n, 0], relay.at[n], sr.at[n], rr.at[n], a_dev))
        direct.append(remote(psum.at[n, b_slot], b_land.at[n], sd.at[n], rd.at[n], b_dev))
        last_hop.append(remote(final_s.at[n], a_land.at[n], sf.at[n], rf.at[n], a_dev))
    normed(y_far, 0)
    swap[0].start()
    for slot, at in ((1, y_up), (2, y_down), (3, y)):
        normed(at, slot)
    swap[1].start()
    sent_w.wait_recv()
    swap[0].wait_recv()
    for n in range(CH):
        project(0, 1, n)
        far[n].start()
    swap[1].wait_recv()
    for n in range(CH):
        project(1, NY, n)
        direct[n].start()
    for n in range(CH):
        a_slot = 1 if n % 2 == 0 else 2
        far[n].wait_recv()
        final_s[n] = (psum[n, a_slot].astype(F32) + relay[n].astype(F32)).astype(BF)
        last_hop[n].start()
    for n in range(CH):
        direct[n].wait_recv()
        last_hop[n].wait_recv()
        t = psum[n, 3].astype(F32) + from_lo[n].astype(F32) + from_hi[n].astype(F32)
        out[:, n * wide : (n + 1) * wide] = t.astype(BF)
    for copy in sent_halo + [sent_w] + c1 + c2 + c3 + c4 + swap + far + direct + last_hop:
        copy.wait_send()


def shards(q, k, v, gate, qt, kt, vt, bl, dl, gain, w):
    D = pltpu.SemaphoreType.DMA
    V = pltpu.VMEM
    hbm = pl.BlockSpec(memory_space=pltpu.HBM)
    vmem = pl.BlockSpec(memory_space=pltpu.VMEM)
    T = q.shape[0]
    wide_in = q.shape[1] + k.shape[1] + v.shape[1]
    args = (q, k, v, gate, qt, kt, vt, bl.T, dl.T, gain.reshape(1, C), w)
    nv = v.shape[1] // C
    r, wide = T // 8, w.shape[1] // CH
    chunk = V((CH, r, wide), BF)
    four = V((CH, NY, r, wide), BF)
    scratch = [V(a.shape, a.dtype) for a in args]
    scratch += [D((len(args),)), V((HALO, wide_in), BF), V(w.shape, BF)]
    scratch += [D((3,)), D((3,)), D((1,)), D((1,))]
    scratch += [
        V((T + 8, wide_in), F32), V((16, T), F32), V((nv, T, C), F32), V((nv, T, C), BF),
        V((nv, C, 2 * C), BF), V((T, nv * C), F32),
    ]
    slots = V((4, C, 2 * C), BF)
    scratch += [slots, V((C, 2 * C), BF), slots, V((C, 2 * C), BF), slots]
    scratch += [V((4, C, C), BF), V((4, C, C), BF)]
    scratch += [D((3,)), D((4,))] * 4
    scratch += [V((2, NY, r, nv * C), BF), V((NY, r, nv * C), BF), four]
    scratch += [chunk] * 4 + [D((2,))] * 2 + [D((CH,))] * 6
    return pl.pallas_call(
        layer_kernel,
        out_shape=jax.ShapeDtypeStruct((r, w.shape[1]), BF),
        in_specs=[hbm] * len(args),
        out_specs=vmem,
        scratch_shapes=scratch,
        compiler_params=pltpu.CompilerParams(
            collective_id=2, has_side_effects=True, vmem_limit_bytes=48 << 20
        ),
        name="layer",
    )(*[pltpu.with_memory_space_constraint(a, pltpu.HBM) for a in args])


def solution(mesh):
    tokens_heads = P("seq", "head")
    placed = (tokens_heads,) * 4 + (P(None, "head"),) * 3 + (tokens_heads,) * 2
    return jax.shard_map(
        shards,
        mesh=mesh,
        in_specs=placed + (P(), P("head", None)),
        out_specs=P(("seq", "head"), None),
        check_vma=False,
    )
```
